256 devices in a mesh: code: 32 (over y, z), dp: 8 (over x, core).
Axes of the slice: x: 4, y: 4, z: 8, core: 2. Of those that a mesh axis runs over, the one named last changes fastest.
Arguments:
- codebook: bfloat16 [262144, 768], P(('code', 'dp')), may hold values from -6 to 6
- weight_in: bfloat16 [768, 1024], replicated, may hold values from -0.21875 to 0.21875
- bias_in: float32 [1024], replicated, may hold values from -3 to 3
- weight_out: bfloat16 [1024, 256], replicated, may hold values from -0.1875 to 0.1875
- bias_out: float32 [256], replicated, may hold values from -3 to 3
- latents: float32 [262144, 256], P(('code', 'dp')), may hold values from -6 to 6
- cotangent: float32 [262144, 256], P(('code', 'dp')), may hold values from -6 to 6
- code_owner: int32 [262144, 1], P(('code', 'dp')), may hold values from 0 to 255; in each aligned block of 1024 rows (0 to 1023, 1024 to 2047, ...) at most 8 rows name the same one
- code_row: int32 [262144], P(('code', 'dp')), may hold values from 0 to 1023
Outputs:
- latent_grad: float32 [262144, 256], P(('code', 'dp'))
- grad_weight_in: float32 [768, 1024], replicated
- grad_bias_in: float32 [1024], replicated
- grad_weight_out: float32 [1024, 256], replicated
- grad_bias_out: float32 [256], replicated
The draws below stay inside these ranges and needn't reach their ends.
Inputs may be any that keep to these rules, and one draw needn't show every extreme that they name: In the rows of one device no owner is named by more than 8 rows, a bound that some block reaches; a latent's code is code_owner * 1024 + code_row.
All inputs are finite; a program needn't handle non-finite values.
Results may differ from the reference program's by a relative error of at most 0.0023.
Values sent between devices are 32-bit elements; how exact they have to be, the bound alone decides.
A program may use at most 128 MiB of HBM per device.

```python
import math
import jax
import jax.numpy as jnp
import numpy as np
from jax import lax

DIM_IN = 768
HIDDEN_SIZE = 1024
CODE_DIM = 256
ROWS_DEV = 1024
LAT_DEV = 1024
VOCAB = 262144
LATENTS = 262144
CAP = 8
DEVICES = 256


def place_ends(array, stream_key, least, largest):
    shape = array.shape
    index_at = [jax.random.randint(jax.random.fold_in(stream_key, axis), (), 0, shape[axis]) for axis in range(len(shape))]
    array = array.at[tuple(index_at)].set(least)
    longest = shape.index(max(shape))
    index_at[longest] = (index_at[longest] + 1) % shape[longest]
    return array.at[tuple(index_at)].set(largest)


def levels(stream_key, shape, split, least, high):
    factor_of = 1.0
    for dim, blocks in split:
        steps = jax.random.uniform(jax.random.fold_in(jax.random.fold_in(stream_key, 6), dim), (blocks,), jnp.float32, least / len(split), high / len(split))
        factor_of = factor_of * jnp.repeat(jnp.exp(steps), shape[dim] // blocks).reshape((-1,) + (1,) * (len(shape) - 1 - dim))
    return factor_of


def cumulative_ranks(amount, slope):
    loads = [(1 << 20) // math.isqrt(grade ** slope) + 1 for grade in range(1, amount + 1)]
    deviation = 1 + sum(loads) // (1 << 30)
    return np.cumsum(np.array([max(1, weight // deviation) for weight in loads]))


def skewed_ids(stream_key, extent, amount, lean):
    grid = cumulative_ranks(amount, lean)
    pick = jax.random.randint(jax.random.fold_in(stream_key, 1), extent, 0, int(grid[amount - 1]))
    standing = jnp.searchsorted(jnp.asarray(grid, jnp.int32), pick, side="right")
    return jax.random.permutation(jax.random.fold_in(stream_key, 2), amount)[standing].astype(jnp.int32)


def routed_block(rng, own, number, rows, number_of, top, bound, slope):
    order = jax.random.permutation(rng, number_of)
    packed, usual = shares(number_of, rows * top, bound, slope, True), shares(number_of, rows * top, bound, slope, False)
    places = jnp.arange(number_of)

    def named(lengths, rotation):
        used = int((lengths > 0).sum())
        fixed = max(1, used // 4)
        moved = fixed + (places - fixed + rotation * (used - fixed)) % max(1, number_of - fixed)
        return jnp.zeros((number_of,), jnp.int32).at[order[jnp.where(places < fixed, places, moved)]].set(jnp.asarray(lengths, jnp.int32))

    lengths = jnp.where(number % 4 == 0, named(packed, number // 4), named(usual, number - number // 4 - 1))
    mixed = jax.random.permutation(jax.random.fold_in(own, 3), number_of)
    giver, taker = mixed[0:number_of // 2 * 2:2], mixed[1:number_of // 2 * 2:2]
    margin = jnp.minimum(lengths[giver] - 1, bound - lengths[taker]) // 2
    margin = jnp.where((giver == order[0]) | (taker == order[0]) | (lengths[taker] == 0), 0, jnp.maximum(margin, 0))
    moved = jax.random.randint(jax.random.fold_in(own, 4), (number_of // 2,), 0, 1 << 20) % (margin + 1)
    lengths = lengths.at[giver].add(-moved).at[taker].add(moved)
    items = jnp.searchsorted(jnp.cumsum(lengths), jnp.arange(rows * top), side="right").astype(jnp.int32)
    table = items.reshape(top, rows).T
    table = table[jax.random.permutation(jax.random.fold_in(own, 1), rows)]
    rotation = jax.random.randint(jax.random.fold_in(own, 2), (rows, 1), 0, top)
    return jnp.take_along_axis(table, (jnp.arange(top)[None, :] + rotation) % top, axis=1)


def shares(number_of, total, limit, lean, full):
    weights = [(1 << 20) // math.isqrt(standing ** lean) + 1 for standing in range(1, number_of + 1)]
    largest = limit if full else min(limit, max(-(-total // number_of), total * weights[0] // sum(weights)))
    least = 1 if total - largest >= number_of - 1 else 0
    given, rest = [largest] + [least] * (number_of - 1), total - largest - least * (number_of - 1)
    while rest > 0:
        free = [i for i in range(1, number_of) if given[i] < largest] or [i for i in range(1, number_of) if given[i] < limit]
        mass, left = sum([weights[i] for i in free]), rest
        for i in free:
            addition = min(limit - given[i], max(1, left * weights[i] // mass), rest)
            given[i] = given[i] + addition
            rest = rest - addition
    return np.array(given)


def centred(rng, dims, scale, most, shards=(), dtype=jnp.bfloat16):
    values = scale * jax.random.normal(rng, dims, jnp.float32)
    if shards:
        values = values * levels(rng, dims, shards, -0.22, 0.18)
    return jnp.clip(values, -most, most).astype(dtype)


def setup_inputs(seed: int = 0) -> dict:
    arg_keys = jax.random.split(jax.random.key(seed), 10)
    codebook = centred(arg_keys[0], (VOCAB, DIM_IN), 1.0, 6.0, ((0, 256),))
    weight_in = centred(arg_keys[1], (DIM_IN, HIDDEN_SIZE), DIM_IN ** -0.5, 0.21875)
    bias_in = centred(arg_keys[2], (HIDDEN_SIZE,), 0.5, 3.0, (), jnp.float32)
    weight_out = centred(arg_keys[3], (HIDDEN_SIZE, CODE_DIM), HIDDEN_SIZE ** -0.5, 0.1875)
    bias_out = centred(arg_keys[4], (CODE_DIM,), 0.5, 3.0, (), jnp.float32)
    latents = centred(arg_keys[5], (LATENTS, CODE_DIM), 1.0, 6.0, ((0, 256),), jnp.float32)
    cotangent = centred(arg_keys[6], (LATENTS, CODE_DIM), 1.0, 6.0, ((0, 256),), jnp.float32)
    code_owner_keys = jax.random.split(jax.random.fold_in(arg_keys[7], 1), LATENTS // LAT_DEV)
    code_owner_turns = jax.random.permutation(jax.random.fold_in(arg_keys[7], 3), LATENTS // LAT_DEV)
    code_owner = jax.vmap(lambda own, number: routed_block(jax.random.fold_in(arg_keys[7], 2), own, number, LAT_DEV, DEVICES, 1, CAP, 2))(code_owner_keys, code_owner_turns).reshape((LATENTS, 1))
    code_row = place_ends(skewed_ids(arg_keys[8], (LATENTS,), ROWS_DEV, 2), jax.random.fold_in(arg_keys[8], 3), 0, ROWS_DEV - 1).astype(jnp.int32)
    return {"codebook": codebook, "weight_in": weight_in, "bias_in": bias_in, "weight_out": weight_out, "bias_out": bias_out, "latents": latents, "cotangent": cotangent, "code_owner": code_owner, "code_row": code_row}


scale_gelu = 0.7978845608028654
cubic_term = 0.044715


def gelu_value(x):
    inner = scale_gelu * (x + cubic_term * x * x * x)
    return 0.5 * x * (1.0 + jnp.tanh(inner))


def gelu_slope(x):
    tangent = jnp.tanh(scale_gelu * (x + cubic_term * x * x * x))
    return 0.5 * (1.0 + tangent) + 0.5 * x * (1.0 - tangent * tangent) * scale_gelu * (1.0 + 3.0 * cubic_term * x * x)


def reference(codebook, weight_in, bias_in, weight_out, bias_out, latents, cotangent, code_owner, code_row):
    index = (code_owner[:, 0] * ROWS_DEV + code_row).astype(jnp.int32)
    blocks = codebook.reshape(VOCAB // ROWS_DEV, ROWS_DEV, DIM_IN)

    def forward(block):
        preact = jnp.dot(block, weight_in, preferred_element_type=jnp.float32) + bias_in
        hidden = gelu_value(preact).astype(jnp.bfloat16)
        return jnp.dot(hidden, weight_out, preferred_element_type=jnp.float32) + bias_out

    projected = lax.map(forward, blocks).reshape(VOCAB, CODE_DIM)
    chosen = jnp.take(projected, index, axis=0)
    residual = chosen - latents
    latent_grad = cotangent - 0.25 * residual
    code_grad = jax.ops.segment_sum(cotangent + residual, index, num_segments=VOCAB)
    grad_blocks = code_grad.reshape(VOCAB // ROWS_DEV, ROWS_DEV, CODE_DIM)

    def backward(carry, items):
        block, grad_block = items
        preact = jnp.dot(block, weight_in, preferred_element_type=jnp.float32) + bias_in
        hidden = gelu_value(preact).astype(jnp.bfloat16)
        code_low = grad_block.astype(jnp.bfloat16)
        gw_out = lax.dot_general(hidden, code_low, (((0,), (0,)), ((), ())), preferred_element_type=jnp.float32)
        back = lax.dot_general(code_low, weight_out, (((1,), (1,)), ((), ())), preferred_element_type=jnp.float32)
        preact_grad = (back * gelu_slope(preact)).astype(jnp.bfloat16)
        gb_in = jnp.sum(preact_grad.astype(jnp.float32), axis=0)
        gw_in = lax.dot_general(block, preact_grad, (((0,), (0,)), ((), ())), preferred_element_type=jnp.float32)
        gb_out = jnp.sum(grad_block, axis=0)
        return (carry[0] + gw_in, carry[1] + gb_in, carry[2] + gw_out, carry[3] + gb_out), None

    start = (jnp.zeros((DIM_IN, HIDDEN_SIZE), jnp.float32), jnp.zeros((HIDDEN_SIZE,), jnp.float32),
             jnp.zeros((HIDDEN_SIZE, CODE_DIM), jnp.float32), jnp.zeros((CODE_DIM,), jnp.float32))
    sums, _ = lax.scan(backward, start, (blocks, grad_blocks))
    return latent_grad, sums[0], sums[1], sums[2], sums[3]
```

```python
import jax
import jax.numpy as jnp
from jax import lax
from jax.experimental import pallas as pl
from jax.experimental.pallas import tpu as pltpu
from jax.sharding import PartitionSpec as P

scale_gelu = 0.7978845608028654
cubic_term = 0.044715

MESH = pl.DeviceIdType.MESH
NX, NY, NZ = 4, 4, 8
F32, BF16 = jnp.float32, jnp.bfloat16


def rows(start, size):
    return pl.ds(pl.multiple_of(start, 8), size)


class Wires:
    def __init__(self, send, recv):
        self.send, self.recv, self.used, self.open = send, recv, 0, []

    def start(self, src, dst, to):
        k = self.used
        self.used += 1
        copy = pltpu.make_async_remote_copy(
            src_ref=src,
            dst_ref=dst,
            send_sem=self.send.at[k],
            recv_sem=self.recv.at[k],
            device_id=to,
            device_id_type=MESH,
        )
        copy.start()
        self.open.append(copy)
        return copy

    def drain(self):
        for copy in self.open:
            copy.wait_send()


AR_WIRES = 2 * (4 + 6 + 6 + 7 + 7 + 6 + 6 + 5) + 14


def position():
    code, dp = lax.axis_index("code"), lax.axis_index("dp")
    return lax.div(dp, 2), lax.div(code, NZ), lax.rem(code, NZ), lax.rem(dp, 2)


def device(x, y, z, c):
    return (y * NZ + z, x * 2 + c)


def ring_peers():
    x, y, z, c = position()
    peers = [device(x, y, z, 1 - c)]
    peers += [device(lax.rem(x + r, NX), y, z, c) for r in range(1, NX)]
    peers += [device(x, lax.rem(y + r, NY), z, c) for r in range(1, NY)]
    peers += [device(x, y, lax.rem(z + r, NZ), c) for r in range(1, NZ)]
    return peers


class Ring:
    def __init__(self, wires, spot, right, left, size):
        self.w, self.p, self.n = wires, spot, size
        self.right, self.left = right, left
        self.h = size // 2

    def chunk(self, step):
        return lax.rem(self.p + step, 4) * self.n

    def scatter_start(self, acc, base, mid, edge):
        n, h, w = self.n, self.h, self.w
        self.acc, self.base, self.mid, self.edge = acc, base, mid, edge
        far, nxt, prv = (base + self.chunk(s) for s in (2, 1, 3))
        self.nxt, self.prv = nxt, prv
        self.far_a = w.start(acc.at[rows(far, h)], mid.at[0], self.right)
        self.far_b = w.start(acc.at[rows(far + h, h)], mid.at[1], self.left)
        self.near_b = w.start(acc.at[rows(nxt + h, h)], edge.at[0, pl.ds(h, h)], self.right)
        self.near_a = w.start(acc.at[rows(prv, h)], edge.at[1, pl.ds(0, h)], self.left)

    def scatter_mid(self):
        h, w, acc = self.h, self.w, self.acc
        self.far_a.wait_recv()
        here = rows(self.nxt, h)
        acc[here, :] = acc[here, :] + self.mid[0]
        self.pass_a = w.start(acc.at[here], self.edge.at[0, pl.ds(0, h)], self.right)
        self.far_b.wait_recv()
        here = rows(self.prv + h, h)
        acc[here, :] = acc[here, :] + self.mid[1]
        self.pass_b = w.start(acc.at[here], self.edge.at[1, pl.ds(h, h)], self.left)

    def scatter_end(self):
        for copy in (self.near_b, self.near_a, self.pass_a, self.pass_b):
            copy.wait_recv()
        mine = self.base + self.chunk(0)
        here = rows(mine, self.n)
        self.acc[here, :] = self.acc[here, :] + (self.edge[0] + self.edge[1])
        return mine

    def gather_start(self, out, base, cols):
        h, w = self.h, self.w
        self.out, self.base, self.cols = out, base, cols
        mine = base + self.chunk(0)
        first, second = (out.at[rows(mine + s, h), cols] for s in (0, h))
        self.right_a = w.start(first, first, self.right)
        self.left_b = w.start(second, second, self.left)
        self.right_b = w.start(second, second, self.right)
        self.left_a = w.start(first, first, self.left)

    def gather_mid(self):
        h, w, out = self.h, self.w, self.out
        self.right_a.wait_recv()
        part = out.at[rows(self.base + self.chunk(3), h), self.cols]
        self.on_a = w.start(part, part, self.right)
        self.left_b.wait_recv()
        part = out.at[rows(self.base + self.chunk(1) + h, h), self.cols]
        self.on_b = w.start(part, part, self.left)

    def gather_near(self):
        self.right_b.wait_recv()
        self.left_a.wait_recv()

    def gather_far(self):
        self.on_a.wait_recv()
        self.on_b.wait_recv()


def reduce_all(wires, grads, bias, out, bias_out, bufs):
    (acc, half, mid1, edge1, mid2, edge2, deep, side0, side1, side2, side3) = bufs
    x, y, z, c = position()
    other = device(x, y, z, 1 - c)
    x_right, x_left = (device(lax.rem(x + s, NX), y, z, c) for s in (1, 3))
    y_right, y_left = (device(x, lax.rem(y + s, NY), z, c) for s in (1, 3))
    along_x, along_y = (x, x_right, x_left), (y, y_right, y_left)
    outer = [Ring(wires, *along_x, 256), Ring(wires, *along_y, 256)]
    inner = [Ring(wires, *along_y, 64), Ring(wires, *along_x, 64)]
    cols = [pl.ds(pl.multiple_of((2 * c + q) * 256, 256), 256) for q in range(2)]
    away = [pl.ds(pl.multiple_of((2 - 2 * c + q) * 256, 256), 256) for q in range(2)]
    order = (2, 1, 3, 0)

    swaps = []
    for step in order:
        for q in range(2):
            here = rows(outer[q].chunk(step), 256)
            swaps.append(wires.start(grads.at[here, away[q]], half.at[q, here], other))
    side = wires.start(bias, side0, other)
    for i, step in enumerate(order):
        for q in range(2):
            here = rows(outer[q].chunk(step), 256)
            swaps[2 * i + q].wait_recv()
            acc[q, here, :] = grads[here, cols[q]] + half[q, here, :]
    for q in range(2):
        outer[q].scatter_start(acc.at[q], 0, mid1.at[q], edge1.at[q])
    side.wait_recv()
    side1[x] = bias[...] + side0[...]
    sides = [
        wires.start(side1.at[x], side1.at[x], device(lax.rem(x + r, NX), y, z, c))
        for r in range(1, NX)
    ]
    for q in range(2):
        outer[q].scatter_mid()
    first = [outer[q].scatter_end() for q in range(2)]
    for q in range(2):
        inner[q].scatter_start(acc.at[q], first[q], mid2.at[q], edge2.at[q])
    for copy in sides:
        copy.wait_recv()
    side2[y] = (side1[0] + side1[1]) + (side1[2] + side1[3])
    sides = [
        wires.start(side2.at[y], side2.at[y], device(x, lax.rem(y + r, NY), z, c))
        for r in range(1, NY)
    ]
    for q in range(2):
        inner[q].scatter_mid()
    second = [inner[q].scatter_end() for q in range(2)]
    columns = [device(x, y, lax.rem(z + r, NZ), c) for r in range(1, NZ)]
    downs = []
    for r in range(1, NZ):
        for q in range(2):
            part = acc.at[q, rows(second[q] + lax.rem(z + r, NZ) * 8, 8)]
            downs.append(wires.start(part, deep.at[q, r - 1], columns[r - 1]))
    for copy in sides:
        copy.wait_recv()
    side3[z] = (side2[0] + side2[1]) + (side2[2] + side2[3])
    sides = [wires.start(side3.at[z], side3.at[z], to) for to in columns]
    for copy in downs:
        copy.wait_recv()
    ups = []
    for q in range(2):
        here = rows(second[q] + z * 8, 8)
        total = acc[q, here, :]
        for r in range(NZ - 1):
            total = total + deep[q, r]
        out[here, cols[q]] = total
        part = out.at[here, cols[q]]
        ups += [wires.start(part, part, to) for to in columns]
    for copy in sides:
        copy.wait_recv()
    total = side3[0]
    for r in range(1, NZ):
        total = total + side3[r]
    bias_out[...] = total
    for copy in ups:
        copy.wait_recv()
    for q in range(2):
        inner[q].gather_start(out, first[q], cols[q])
    for q in range(2):
        inner[q].gather_mid()
    for q in range(2):
        inner[q].gather_near()
        inner[q].gather_far()
    for q in range(2):
        outer[q].gather_start(out, 0, cols[q])
    backs = []

    def back(q, start, size):
        part = out.at[rows(start, size), cols[q]]
        backs.append(wires.start(part, part, other))

    for q in range(2):
        back(q, outer[q].chunk(0), 256)
    for q in range(2):
        outer[q].gather_mid()
    for q in range(2):
        outer[q].gather_near()
        back(q, outer[q].chunk(3), 256)
        back(q, outer[q].chunk(1), 256)
    for q in range(2):
        outer[q].on_a.wait_recv()
        back(q, outer[q].chunk(2), 128)
        outer[q].on_b.wait_recv()
        back(q, outer[q].chunk(2) + 128, 128)
    for copy in backs:
        copy.wait_recv()


AR_BUFS = [
    pltpu.VMEM((2, 1024, 256), F32),
    pltpu.VMEM((2, 1024, 256), F32),
    pltpu.VMEM((2, 2, 128, 256), F32),
    pltpu.VMEM((2, 2, 256, 256), F32),
    pltpu.VMEM((2, 2, 32, 256), F32),
    pltpu.VMEM((2, 2, 64, 256), F32),
    pltpu.VMEM((2, 7, 8, 256), F32),
    pltpu.VMEM((8, 256), F32),
    pltpu.VMEM((4, 8, 256), F32),
    pltpu.VMEM((4, 8, 256), F32),
    pltpu.VMEM((8, 8, 256), F32),
]


def meet(peers):
    barrier = pltpu.get_barrier_semaphore()
    for peer in peers:
        pl.semaphore_signal(barrier, inc=1, device_id=peer, device_id_type=MESH)
    pl.semaphore_wait(barrier, len(peers))


def reduce_kernel(grads, bias, out, bias_out, *scratch):
    meet(ring_peers())
    wires = Wires(scratch[-2], scratch[-1])
    reduce_all(wires, grads, bias, out, bias_out, scratch[:-2])
    wires.drain()
    assert wires.used == AR_WIRES, wires.used


def reduce_grads(grads, bias):
    vmem = pl.BlockSpec(memory_space=pltpu.VMEM)
    return pl.pallas_call(
        reduce_kernel,
        out_shape=(
            jax.ShapeDtypeStruct((1024, 1024), F32),
            jax.ShapeDtypeStruct((8, 256), F32),
        ),
        in_specs=[vmem, vmem],
        out_specs=(vmem, vmem),
        scratch_shapes=AR_BUFS
        + [pltpu.SemaphoreType.DMA((AR_WIRES,)), pltpu.SemaphoreType.DMA((AR_WIRES,))],
        compiler_params=pltpu.CompilerParams(
            collective_id=1, has_side_effects=True, vmem_limit_bytes=60 * 2**20
        ),
    )(grads, bias)


def in_blocks(array, dim, size):
    before, after = (array.shape[:dim], array.shape[dim + 1 :])
    return jnp.moveaxis(array.reshape(*before, size, -1, *after), dim, 0)


def in_order(tiles, dim):
    shape = list(tiles.shape[1:])
    shape[dim] *= tiles.shape[0]
    return jnp.moveaxis(tiles, 0, dim).reshape(shape)


def exchange_both(array, axis, axes, splits, concats):
    sizes = [lax.axis_size(a) for a in axes]
    tiles = in_blocks(array, splits[0], sizes[0])
    tiles = jnp.moveaxis(in_blocks(tiles, splits[1] + 1, sizes[1]), 0, 1)
    inside = tiles.shape[2:]
    tiles = tiles.reshape(-1, *inside)
    tiles = lax.all_to_all(tiles, axis, split_axis=0, concat_axis=0, tiled=True)
    tiles = in_order(tiles.reshape(*sizes, *inside), concats[0] + 1)
    return in_order(tiles, concats[1])


def gelu_value(x):
    inner = scale_gelu * (x + cubic_term * x * x * x)
    return 0.5 * x * (1.0 + jnp.tanh(inner))


def gelu_slope(x):
    tangent = jnp.tanh(scale_gelu * (x + cubic_term * x * x * x))
    return 0.5 * (1.0 + tangent) + 0.5 * x * (1.0 - tangent * tangent) * scale_gelu * (
        1.0 + 3.0 * cubic_term * x * x
    )


def per_device(
    codebook, weight_in, bias_in, weight_out, bias_out, latents, cotangent, code_owner, code_row
):
    preact = jnp.dot(codebook, weight_in, preferred_element_type=jnp.float32) + bias_in
    hidden = gelu_value(preact).astype(jnp.bfloat16)
    projected = jnp.dot(hidden, weight_out, preferred_element_type=jnp.float32) + bias_out
    n_code = lax.axis_size("code")
    n_data = lax.axis_size("dp")
    devices = n_code * n_data
    owners = code_owner[:, 0]
    count = owners.shape[0]
    width = latents.shape[1]
    capacity = max(2, 2 * count // devices)
    position = jnp.arange(count, dtype=jnp.int32)
    same = (owners[:, None] == owners[None, :]) & (position[None, :] < position[:, None])
    ranks = jnp.sum(same.astype(jnp.int32), axis=1)
    slots = owners * capacity + ranks
    wanted = jnp.full((devices * capacity,), -1, jnp.int32).at[slots].set(code_row)
    wanted = exchange_both(
        wanted.reshape(n_code, n_data, capacity), ("code", "dp"), ("code", "dp"), (0, 1), (0, 1)
    )
    valid = wanted >= 0
    row_ids = jnp.maximum(wanted, 0).reshape(-1)
    outgoing = (
        jnp.zeros((devices * capacity, width), jnp.float32).at[slots].set(cotangent - latents)
    )
    incoming = exchange_both(
        outgoing.reshape(n_code, n_data, capacity, width),
        ("code", "dp"),
        ("code", "dp"),
        (0, 1),
        (0, 1),
    )
    picked = jnp.take(projected, row_ids, axis=0).reshape(n_code, n_data, capacity, width)
    picked = jnp.where(valid[..., None], picked, 0.0)
    answers = exchange_both(picked, ("code", "dp"), ("code", "dp"), (0, 1), (0, 1))
    chosen = jnp.take(answers.reshape(devices * capacity, width), slots, axis=0)
    latent_grad = cotangent - 0.25 * (chosen - latents)
    code_grad = jax.ops.segment_sum(
        (incoming + picked).reshape(devices * capacity, width),
        row_ids,
        num_segments=projected.shape[0],
    )
    code_low = code_grad.astype(jnp.bfloat16)
    gw_out = lax.dot_general(
        hidden, code_low, (((0,), (0,)), ((), ())), preferred_element_type=jnp.float32
    )
    back = lax.dot_general(
        code_low, weight_out, (((1,), (1,)), ((), ())), preferred_element_type=jnp.float32
    )
    preact_grad = (back * gelu_slope(preact)).astype(jnp.bfloat16)
    gb_in = jnp.sum(preact_grad.astype(jnp.float32), axis=0)
    gw_in = lax.dot_general(
        codebook, preact_grad, (((0,), (0,)), ((), ())), preferred_element_type=jnp.float32
    )
    gb_out = jnp.sum(code_grad, axis=0)
    wide = gw_out.reshape(4, 256, 256).transpose(1, 0, 2).reshape(256, 1024)
    grads = jnp.concatenate([gw_in, wide], axis=0)
    bias = jnp.concatenate(
        [gb_in.reshape(4, 256), gb_out[None], jnp.zeros((3, 256), jnp.float32)], axis=0
    )
    grads, bias = reduce_grads(grads, bias)
    gw_in = grads[:768]
    gw_out = grads[768:].reshape(256, 4, 256).transpose(1, 0, 2).reshape(1024, 256)
    return (latent_grad, gw_in, bias[:4].reshape(1024), gw_out, bias[4])


def solution(mesh):
    placed = (
        P(("code", "dp"), None),
        P(),
        P(),
        P(),
        P(),
        P(("code", "dp"), None),
        P(("code", "dp"), None),
        P(("code", "dp"), None),
        P(("code", "dp")),
    )
    return jax.shard_map(
        per_device,
        mesh=mesh,
        in_specs=placed,
        out_specs=(P(("code", "dp"), None), P(), P(), P(), P()),
        check_vma=False,
    )
```

```python
import jax
import jax.numpy as jnp
from jax import lax
from jax.experimental import pallas as pl
from jax.experimental.pallas import tpu as pltpu
from jax.sharding import PartitionSpec as P

scale_gelu = 0.7978845608028654
cubic_term = 0.044715

MESH = pl.DeviceIdType.MESH
NX, NY, NZ = 4, 4, 8
CAP, DEVICES = 8, 256
F32, BF16 = jnp.float32, jnp.bfloat16


def rows(start, size):
    return pl.ds(pl.multiple_of(start, 8), size)


class Wires:
    def __init__(self, send, recv):
        self.send, self.recv, self.used, self.open = send, recv, 0, []

    def start(self, src, dst, to):
        k = self.used
        self.used += 1
        copy = pltpu.make_async_remote_copy(
            src_ref=src,
            dst_ref=dst,
            send_sem=self.send.at[k],
            recv_sem=self.recv.at[k],
            device_id=to,
            device_id_type=MESH,
        )
        copy.start()
        self.open.append(copy)
        return copy

    def drain(self):
        for copy in self.open:
            copy.wait_send()


AR_WIRES = 2 * (4 + 6 + 6 + 7 + 7 + 6 + 6 + 5) + 14


def position():
    code, dp = lax.axis_index("code"), lax.axis_index("dp")
    return lax.div(dp, 2), lax.div(code, NZ), lax.rem(code, NZ), lax.rem(dp, 2)


def device(x, y, z, c):
    return (y * NZ + z, x * 2 + c)


def ring_peers():
    x, y, z, c = position()
    peers = [device(x, y, z, 1 - c)]
    peers += [device(lax.rem(x + r, NX), y, z, c) for r in range(1, NX)]
    peers += [device(x, lax.rem(y + r, NY), z, c) for r in range(1, NY)]
    peers += [device(x, y, lax.rem(z + r, NZ), c) for r in range(1, NZ)]
    return peers


class Ring:
    def __init__(self, wires, spot, right, left, size):
        self.w, self.p, self.n = wires, spot, size
        self.right, self.left = right, left
        self.h = size // 2

    def chunk(self, step):
        return lax.rem(self.p + step, 4) * self.n

    def scatter_start(self, acc, base, mid, edge):
        n, h, w = self.n, self.h, self.w
        self.acc, self.base, self.mid, self.edge = acc, base, mid, edge
        far, nxt, prv = (base + self.chunk(s) for s in (2, 1, 3))
        self.nxt, self.prv = nxt, prv
        self.far_a = w.start(acc.at[rows(far, h)], mid.at[0], self.right)
        self.far_b = w.start(acc.at[rows(far + h, h)], mid.at[1], self.left)
        self.near_b = w.start(acc.at[rows(nxt + h, h)], edge.at[0, pl.ds(h, h)], self.right)
        self.near_a = w.start(acc.at[rows(prv, h)], edge.at[1, pl.ds(0, h)], self.left)

    def scatter_mid(self):
        h, w, acc = self.h, self.w, self.acc
        self.far_a.wait_recv()
        here = rows(self.nxt, h)
        acc[here, :] = acc[here, :] + self.mid[0]
        self.pass_a = w.start(acc.at[here], self.edge.at[0, pl.ds(0, h)], self.right)
        self.far_b.wait_recv()
        here = rows(self.prv + h, h)
        acc[here, :] = acc[here, :] + self.mid[1]
        self.pass_b = w.start(acc.at[here], self.edge.at[1, pl.ds(h, h)], self.left)

    def scatter_end(self):
        for copy in (self.near_b, self.near_a, self.pass_a, self.pass_b):
            copy.wait_recv()
        mine = self.base + self.chunk(0)
        here = rows(mine, self.n)
        self.acc[here, :] = self.acc[here, :] + (self.edge[0] + self.edge[1])
        return mine

    def gather_start(self, out, base, cols):
        h, w = self.h, self.w
        self.out, self.base, self.cols = out, base, cols
        mine = base + self.chunk(0)
        first, second = (out.at[rows(mine + s, h), cols] for s in (0, h))
        self.right_a = w.start(first, first, self.right)
        self.left_b = w.start(second, second, self.left)
        self.right_b = w.start(second, second, self.right)
        self.left_a = w.start(first, first, self.left)

    def gather_mid(self):
        h, w, out = self.h, self.w, self.out
        self.right_a.wait_recv()
        part = out.at[rows(self.base + self.chunk(3), h), self.cols]
        self.on_a = w.start(part, part, self.right)
        self.left_b.wait_recv()
        part = out.at[rows(self.base + self.chunk(1) + h, h), self.cols]
        self.on_b = w.start(part, part, self.left)

    def gather_near(self):
        self.right_b.wait_recv()
        self.left_a.wait_recv()

    def gather_far(self):
        self.on_a.wait_recv()
        self.on_b.wait_recv()


def rings(wires):
    x, y, z, c = position()
    x_right, x_left = (device(lax.rem(x + s, NX), y, z, c) for s in (1, 3))
    y_right, y_left = (device(x, lax.rem(y + s, NY), z, c) for s in (1, 3))
    along_x, along_y = (x, x_right, x_left), (y, y_right, y_left)
    outer = [Ring(wires, *along_x, 256), Ring(wires, *along_y, 256)]
    inner = [Ring(wires, *along_y, 64), Ring(wires, *along_x, 64)]
    return outer, inner


ORDER = (2, 1, 3, 0)


def swap_start(wires, grads, bufs):
    half = bufs[1]
    x, y, z, c = position()
    away = [pl.ds(pl.multiple_of((2 - 2 * c + q) * 256, 256), 256) for q in range(2)]
    outer, _ = rings(wires)
    swaps = []
    for step in ORDER:
        for q in range(2):
            here = rows(outer[q].chunk(step), 256)
            swaps.append(
                wires.start(grads.at[here, away[q]], half.at[q, here], device(x, y, z, 1 - c))
            )
    return swaps


def reduce_all(wires, swaps, grads, bias, out, bias_out, bufs, between):
    (acc, half, mid1, edge1, mid2, edge2, deep, side0, side1, side2, side3) = bufs
    x, y, z, c = position()
    other = device(x, y, z, 1 - c)
    outer, inner = rings(wires)
    cols = [pl.ds(pl.multiple_of((2 * c + q) * 256, 256), 256) for q in range(2)]
    side = wires.start(bias, side0, other)
    for i, step in enumerate(ORDER):
        for q in range(2):
            here = rows(outer[q].chunk(step), 256)
            swaps[2 * i + q].wait_recv()
            acc[q, here, :] = grads[here, cols[q]] + half[q, here, :]
    for q in range(2):
        outer[q].scatter_start(acc.at[q], 0, mid1.at[q], edge1.at[q])
    side.wait_recv()
    side1[x] = bias[...] + side0[...]
    sides = [
        wires.start(side1.at[x], side1.at[x], device(lax.rem(x + r, NX), y, z, c))
        for r in range(1, NX)
    ]
    for q in range(2):
        outer[q].scatter_mid()
    first = [outer[q].scatter_end() for q in range(2)]
    for q in range(2):
        inner[q].scatter_start(acc.at[q], first[q], mid2.at[q], edge2.at[q])
    for copy in sides:
        copy.wait_recv()
    side2[y] = (side1[0] + side1[1]) + (side1[2] + side1[3])
    sides = [
        wires.start(side2.at[y], side2.at[y], device(x, lax.rem(y + r, NY), z, c))
        for r in range(1, NY)
    ]
    for q in range(2):
        inner[q].scatter_mid()
    second = [inner[q].scatter_end() for q in range(2)]
    columns = [device(x, y, lax.rem(z + r, NZ), c) for r in range(1, NZ)]
    downs = []
    for r in range(1, NZ):
        for q in range(2):
            part = acc.at[q, rows(second[q] + lax.rem(z + r, NZ) * 8, 8)]
            downs.append(wires.start(part, deep.at[q, r - 1], columns[r - 1]))
    for copy in sides:
        copy.wait_recv()
    side3[z] = (side2[0] + side2[1]) + (side2[2] + side2[3])
    sides = [wires.start(side3.at[z], side3.at[z], to) for to in columns]
    for copy in downs:
        copy.wait_recv()
    ups = []
    for q in range(2):
        here = rows(second[q] + z * 8, 8)
        total = acc[q, here, :]
        for r in range(NZ - 1):
            total = total + deep[q, r]
        out[here, cols[q]] = total
        part = out.at[here, cols[q]]
        ups += [wires.start(part, part, to) for to in columns]
    for copy in sides:
        copy.wait_recv()
    total = side3[0]
    for r in range(1, NZ):
        total = total + side3[r]
    bias_out[...] = total
    for copy in ups:
        copy.wait_recv()
    for q in range(2):
        inner[q].gather_start(out, first[q], cols[q])
    for q in range(2):
        inner[q].gather_mid()
    for q in range(2):
        inner[q].gather_near()
        inner[q].gather_far()
    for q in range(2):
        outer[q].gather_start(out, 0, cols[q])
    backs = []

    def back(q, start, size):
        part = out.at[rows(start, size), cols[q]]
        backs.append(wires.start(part, part, other))

    for q in range(2):
        back(q, outer[q].chunk(0), 256)
    for q in range(2):
        outer[q].gather_mid()
    for q in range(2):
        outer[q].gather_near()
        back(q, outer[q].chunk(3), 256)
        back(q, outer[q].chunk(1), 256)
    between()
    for q in range(2):
        outer[q].on_a.wait_recv()
        back(q, outer[q].chunk(2), 128)
        outer[q].on_b.wait_recv()
        back(q, outer[q].chunk(2) + 128, 128)
    for copy in backs:
        copy.wait_recv()


AR_BUFS = [
    pltpu.VMEM((2, 1024, 256), F32),
    pltpu.VMEM((2, 1024, 256), F32),
    pltpu.VMEM((2, 2, 128, 256), F32),
    pltpu.VMEM((2, 2, 256, 256), F32),
    pltpu.VMEM((2, 2, 32, 256), F32),
    pltpu.VMEM((2, 2, 64, 256), F32),
    pltpu.VMEM((2, 7, 8, 256), F32),
    pltpu.VMEM((8, 256), F32),
    pltpu.VMEM((4, 8, 256), F32),
    pltpu.VMEM((4, 8, 256), F32),
    pltpu.VMEM((8, 8, 256), F32),
]


def linear(x, y, z, c):
    return ((y * NZ + z) * NX + x) * 2 + c


def partner(i):
    x, y, z, c = position()
    z = lax.rem(z + lax.rem(i, 8), NZ)
    x = lax.rem(x + lax.rem(lax.div(i, 8), 4), NX)
    y = lax.rem(y + lax.rem(lax.div(i, 32), 4), NY)
    c = lax.rem(c + lax.div(i, 128), 2)
    return device(x, y, z, c), linear(x, y, z, c)


def greet(peers, sem):
    for peer in peers:
        pl.semaphore_signal(sem, inc=1, device_id=peer, device_id_type=MESH)


def spread(source, target, send, recv):
    me = linear(*position())

    def one(i, carry):
        to, index = partner(i)
        pltpu.make_async_remote_copy(
            src_ref=source.at[index],
            dst_ref=target.at[me],
            send_sem=send,
            recv_sem=recv,
            device_id=to,
            device_id_type=MESH,
        ).start()
        return carry

    lax.fori_loop(1, DEVICES, one, 0)
    target[me] = source[me]
    to, _ = partner(1)
    return pltpu.make_async_remote_copy(
        src_ref=source.at[pl.ds(0, DEVICES - 1)],
        dst_ref=target.at[pl.ds(0, DEVICES - 1)],
        send_sem=send,
        recv_sem=recv,
        device_id=to,
        device_id_type=MESH,
    )


def dot(a, b):
    return jnp.dot(a, b, preferred_element_type=F32)


def halves(value):
    high = value.astype(BF16)
    low = (value - high.astype(F32)).astype(BF16)
    return jnp.concatenate([high, low], axis=1)


def joined(value):
    return value[:, :256] + value[:, 256:]


def upright(row):
    return jnp.transpose(jnp.broadcast_to(row, (128, row.shape[1])))


def iota(shape, dim):
    return lax.broadcasted_iota(jnp.int32, shape, dim).astype(F32)


def one_hot(condition):
    return jnp.where(condition, 1.0, 0.0).astype(BF16)


def whole_kernel(
    codebook_h, weight_in_h, bias_in, weight_out_h, bias_out, latents, cotangent, owner, code,
    latent_grad, out, side_out,
    codebook, weight_in, weight_out, slot_col, values, send_a, recv_a, send_b, recv_b, ids_out, ids_in,
    slope, hidden_t, codebook_t, weight_out_t, projected, base, picks, code_low, grads, side,
    load, ids_s, ids_r, a_s, a_r, b_s, b_r, near_a, near_b, wire_s, wire_r, *bufs,
):
    x, y, z, c = position()
    loads = [
        pltpu.make_async_copy(src, dst, load.at[i])
        for i, (src, dst) in enumerate(
            ((codebook_h, codebook), (weight_in_h, weight_in), (weight_out_h, weight_out))
        )
    ]
    for copy in loads:
        copy.start()
    barrier = pltpu.get_barrier_semaphore()
    row_peers = [
        device(lax.rem(x + r, NX), y, z, lax.rem(c + s, 2))
        for r in range(NX) for s in range(2) if r + s
    ]
    y_peers = [device(x, lax.rem(y + r, NY), z, c) for r in range(1, NY)]
    z_peers = [device(x, y, lax.rem(z + r, NZ), c) for r in range(1, NZ)]
    line_peers = row_peers + y_peers + z_peers
    greet(line_peers, barrier)

    owner_row = owner[...].astype(F32)
    code_row = code[...].astype(F32) + 1.0
    owner_col = upright(owner_row)
    lower = iota((128, 128), 0) < iota((128, 128), 1)
    ranks = []
    for i in range(8):
        name = owner_row[:, 128 * i : 128 * i + 128]
        count = jnp.where((owner_col[128 * i : 128 * i + 128] == name) & lower, 1.0, 0.0)
        for j in range(i):
            count += jnp.where(owner_col[128 * j : 128 * j + 128] == name, 1.0, 0.0)
        ranks.append(jnp.sum(count, axis=0, keepdims=True))
    rank_row = jnp.concatenate(ranks, axis=1)
    slot_row = owner_row * CAP + rank_row
    slot_col[...] = upright(slot_row)
    pl.semaphore_wait(barrier, len(line_peers))
    greet(row_peers, near_a)

    rank_col = upright(rank_row)
    code_col = upright(code_row)
    code_high = jnp.floor(code_col * (1.0 / 32))
    mine = rank_col == iota((1024, 128), 1)
    digits = jnp.concatenate(
        [
            jnp.where(mine, code_high, 0.0).astype(BF16),
            jnp.where(mine, code_col - 32.0 * code_high, 0.0).astype(BF16),
        ],
        axis=1,
    )
    named = dot(one_hot(owner_row == iota((256, 1024), 0)), digits)
    ids_out[:, 0, :] = named[:, :128] * 32.0 + named[:, 128:] - 1.0
    values[pl.ds(0, 1024), :] = halves(cotangent[...] - latents[...])
    pl.semaphore_wait(near_a, len(row_peers))
    greet(y_peers, near_b)

    def arrange(i, carry):
        hot = one_hot(slot_row == iota((256, 1024), 0) + (i * 256).astype(F32))
        block = joined(dot(hot, values[pl.ds(0, 1024), :]))
        send_a[pl.ds(i * 32, 32)] = block.reshape(32, CAP, 256)
        return carry

    lax.fori_loop(0, 8, arrange, 0)
    pl.semaphore_wait(near_b, len(y_peers))
    ids_all = spread(ids_out, ids_in, ids_s, ids_r)
    rows_all = spread(send_a, recv_a, a_s, a_r)

    for copy in loads:
        copy.wait()
    weight_out_t[...] = jnp.transpose(weight_out[...].astype(F32)).astype(BF16)

    def forward(i, carry):
        here = rows(i * 256, 256)
        block = codebook[here, :]
        pre = dot(block, weight_in[...]) + bias_in[...]
        tangent = jnp.tanh(scale_gelu * (pre + cubic_term * pre * pre * pre))
        value = 0.5 * pre * (1.0 + tangent)
        slope[here, :] = 0.5 * (1.0 + tangent) + 0.5 * pre * (
            1.0 - tangent * tangent
        ) * scale_gelu * (1.0 + 3.0 * cubic_term * pre * pre)
        hidden = value.astype(BF16)
        cols = pl.ds(pl.multiple_of(i * 256, 256), 256)
        hidden_t[:, cols] = jnp.transpose(value).astype(BF16)
        codebook_t[:, cols] = jnp.transpose(block.astype(F32)).astype(BF16)
        block = dot(hidden, weight_out[...]) + bias_out[...]
        base[here, :] = block
        projected[here, :] = halves(block)
        return carry

    lax.fori_loop(0, 4, forward, 0)

    ids_all.wait_recv()
    ids = ids_in[:, 0, :]
    ids_t = jnp.transpose(ids)
    ones = jnp.ones((256, 128), BF16)
    for j in range(CAP):
        hot = one_hot(ids[:, j : j + 1] == iota((256, 1024), 1))
        send_b[:, j, :] = joined(dot(hot, projected[...]))
        for i in range(4):
            hot = one_hot(ids_t[j : j + 1, :] == iota((256, 256), 0) + 256.0 * i)
            picks[j, pl.ds(i * 256, 256), :] = hot
    for i in range(4):
        here = pl.ds(i * 256, 256)
        count = dot(picks[0, here, :], ones)
        for j in range(1, CAP):
            count += dot(picks[j, here, :], ones)
        base[here, :] = base[here, :] * jnp.concatenate([count, count], axis=1)

    rows_all.wait_recv()
    back_all = spread(send_b, recv_b, b_s, b_r)
    for j in range(CAP):
        values[pl.ds(j * 256, 256), :] = halves(recv_a[:, j, :])
    side_rows = []
    for i in range(4):
        here = pl.ds(i * 256, 256)
        total = dot(picks[0, here, :], values[pl.ds(0, 256), :])
        for j in range(1, CAP):
            total += dot(picks[j, here, :], values[pl.ds(j * 256, 256), :])
        total = base[here, :] + joined(total)
        code_low[here, :] = total.astype(BF16)
        side_rows.append(jnp.sum(total, axis=0, keepdims=True))
    side[...] = jnp.zeros((8, 256), F32)
    side[4:5, :] = (side_rows[0] + side_rows[1]) + (side_rows[2] + side_rows[3])

    def gradient(b):
        cols = pl.ds(pl.multiple_of(b * 256, 256), 256)
        back = dot(code_low[...], weight_out_t[:, cols])
        low = (back * slope[:, cols]).astype(BF16)
        side[pl.ds(b, 1), :] = jnp.sum(low.astype(F32), axis=0, keepdims=True)
        grads[pl.ds(0, 768), cols] = dot(codebook_t[...], low)
        grads[pl.ds(768, 256), cols] = dot(hidden_t[rows(b * 256, 256), :], code_low[...])

    for q in range(2):
        gradient(2 - 2 * c + q)
    wires = Wires(wire_s, wire_r)
    swaps = swap_start(wires, grads, bufs)
    for q in range(2):
        gradient(2 * c + q)

    def chosen():
        back_all.wait_recv()
        for j in range(8):
            values[pl.ds(j * 256, 256), :] = halves(recv_b[pl.ds(j * 32, 32)].reshape(256, 256))

        def pick(i, carry):
            here = rows(i * 256, 256)
            slot = slot_col[here, :]
            total = jnp.zeros((256, 512), F32)
            for j in range(8):
                hot = jnp.concatenate(
                    [one_hot(slot == iota((256, 128), 1) + float(j * 256 + k * 128)) for k in range(2)],
                    axis=1,
                )
                total += dot(hot, values[pl.ds(j * 256, 256), :])
            residual = joined(total) - latents[here, :]
            latent_grad[here, :] = cotangent[here, :] - 0.25 * residual
            return carry

        lax.fori_loop(0, 4, pick, 0)

    reduce_all(wires, swaps, grads, side, out, side_out, bufs, chosen)
    wires.drain()
    ids_all.wait_send()
    rows_all.wait_send()
    back_all.wait_send()
    assert wires.used == AR_WIRES, wires.used


def whole(codebook, weight_in, bias_in, weight_out, bias_out, latents, cotangent, owner, code):
    vmem, anywhere = (pl.BlockSpec(memory_space=m) for m in (pltpu.VMEM, pl.ANY))
    dma, plain = pltpu.SemaphoreType.DMA, pltpu.SemaphoreType.REGULAR
    scratch = [
        pltpu.VMEM((1024, 768), BF16),
        pltpu.VMEM((768, 1024), BF16),
        pltpu.VMEM((1024, 256), BF16),
        pltpu.VMEM((1024, 128), F32),
        pltpu.VMEM((2048, 512), BF16),
    ]
    scratch += [pltpu.VMEM((DEVICES, CAP, 256), F32)] * 4
    scratch += [pltpu.VMEM((DEVICES, 1, 128), F32)] * 2
    scratch += [
        pltpu.VMEM((1024, 1024), F32),
        pltpu.VMEM((1024, 1024), BF16),
        pltpu.VMEM((768, 1024), BF16),
        pltpu.VMEM((256, 1024), BF16),
        pltpu.VMEM((1024, 512), BF16),
        pltpu.VMEM((1024, 256), F32),
        pltpu.VMEM((CAP, 1024, 256), BF16),
        pltpu.VMEM((1024, 256), BF16),
        pltpu.VMEM((1024, 1024), F32),
        pltpu.VMEM((8, 256), F32),
        dma((3,)), dma, dma, dma, dma, dma, dma, plain, plain,
        dma((AR_WIRES,)), dma((AR_WIRES,)),
    ]
    return pl.pallas_call(
        whole_kernel,
        out_shape=(
            jax.ShapeDtypeStruct((1024, 256), F32),
            jax.ShapeDtypeStruct((1024, 1024), F32),
            jax.ShapeDtypeStruct((8, 256), F32),
        ),
        in_specs=[anywhere, anywhere, vmem, anywhere, vmem, vmem, vmem, vmem, vmem],
        out_specs=(vmem, vmem, vmem),
        scratch_shapes=scratch + AR_BUFS,
        compiler_params=pltpu.CompilerParams(
            collective_id=1, has_side_effects=True, vmem_limit_bytes=62 * 2**20
        ),
    )(codebook, weight_in, bias_in, weight_out, bias_out, latents, cotangent, owner, code)


def per_device(
    codebook, weight_in, bias_in, weight_out, bias_out, latents, cotangent, code_owner, code_row
):
    latent_grad, grads, side = whole(
        codebook, weight_in, bias_in[None], weight_out, bias_out[None], latents, cotangent,
        code_owner.reshape(1, 1024), code_row.reshape(1, 1024),
    )
    gw_in = grads[:768]
    gw_out = grads[768:].reshape(256, 4, 256).transpose(1, 0, 2).reshape(1024, 256)
    return (latent_grad, gw_in, side[:4].reshape(1024), gw_out, side[4])


def solution(mesh):
    placed = (
        P(("code", "dp"), None),
        P(),
        P(),
        P(),
        P(),
        P(("code", "dp"), None),
        P(("code", "dp"), None),
        P(("code", "dp"), None),
        P(("code", "dp")),
    )
    return jax.shard_map(
        per_device,
        mesh=mesh,
        in_specs=placed,
        out_specs=(P(("code", "dp"), None), P(), P(), P(), P()),
        check_vma=False,
    )
```

```python
import jax
import jax.numpy as jnp
from jax import lax
from jax.experimental import pallas as pl
from jax.experimental.pallas import tpu as pltpu
from jax.sharding import PartitionSpec as P

scale_gelu = 0.7978845608028654
cubic_term = 0.044715


MESH = pl.DeviceIdType.MESH
NX, NY, NZ = 4, 4, 8
CAP, DEVICES, GROUPS, CODES = 8, 256, 8, 32
PACE = 4
LANES = 128
F32, BF16 = jnp.float32, jnp.bfloat16


def rows(start, size):
    return pl.ds(pl.multiple_of(start, 8), size)


class Wires:
    def __init__(self, send, recv):
        self.send, self.recv, self.used, self.open = send, recv, 0, []

    def start(self, src, dst, to):
        k = self.used
        self.used += 1
        copy = pltpu.make_async_remote_copy(
            src_ref=src,
            dst_ref=dst,
            send_sem=self.send.at[k],
            recv_sem=self.recv.at[k],
            device_id=to,
            device_id_type=MESH,
        )
        copy.start()
        self.open.append(copy)
        return copy

    def drain(self):
        for copy in self.open:
            copy.wait_send()


FLOWS = 4
AR_WIRES = FLOWS * (4 + 6 + 6 + 7 + 7 + 6 + 6 + 5) + 14


def position():
    code, dp = lax.axis_index("code"), lax.axis_index("dp")
    return lax.div(dp, 2), lax.div(code, NZ), lax.rem(code, NZ), lax.rem(dp, 2)


def device(x, y, z, c):
    return (y * NZ + z, x * 2 + c)


class Ring:
    def __init__(self, wires, spot, right, left, size):
        self.w, self.p, self.n = wires, spot, size
        self.right, self.left = right, left
        self.h = size // 2

    def chunk(self, step):
        return lax.rem(self.p + step, 4) * self.n

    def scatter_start(self, acc, base, mid, edge):
        n, h, w = self.n, self.h, self.w
        self.acc, self.base, self.mid, self.edge = acc, base, mid, edge
        far, nxt, prv = (base + self.chunk(s) for s in (2, 1, 3))
        self.nxt, self.prv = nxt, prv
        self.far_a = w.start(acc.at[rows(far, h)], mid.at[0], self.right)
        self.far_b = w.start(acc.at[rows(far + h, h)], mid.at[1], self.left)
        self.near_b = w.start(acc.at[rows(nxt + h, h)], edge.at[0, pl.ds(h, h)], self.right)
        self.near_a = w.start(acc.at[rows(prv, h)], edge.at[1, pl.ds(0, h)], self.left)

    def scatter_mid(self):
        h, w, acc = self.h, self.w, self.acc
        self.far_a.wait_recv()
        here = rows(self.nxt, h)
        acc[here, :] = acc[here, :] + self.mid[0]
        self.pass_a = w.start(acc.at[here], self.edge.at[0, pl.ds(0, h)], self.right)
        self.far_b.wait_recv()
        here = rows(self.prv + h, h)
        acc[here, :] = acc[here, :] + self.mid[1]
        self.pass_b = w.start(acc.at[here], self.edge.at[1, pl.ds(h, h)], self.left)

    def scatter_end(self):
        for copy in (self.near_b, self.near_a, self.pass_a, self.pass_b):
            copy.wait_recv()
        mine = self.base + self.chunk(0)
        here = rows(mine, self.n)
        self.acc[here, :] = self.acc[here, :] + (self.edge[0] + self.edge[1])
        return mine

    def gather_start(self, out, base, cols):
        h, w = self.h, self.w
        self.out, self.base, self.cols = out, base, cols
        mine = base + self.chunk(0)
        first, second = (out.at[rows(mine + s, h), cols] for s in (0, h))
        self.right_a = w.start(first, first, self.right)
        self.left_b = w.start(second, second, self.left)
        self.right_b = w.start(second, second, self.right)
        self.left_a = w.start(first, first, self.left)

    def gather_mid(self):
        h, w, out = self.h, self.w, self.out
        self.right_a.wait_recv()
        part = out.at[rows(self.base + self.chunk(3), h), self.cols]
        self.on_a = w.start(part, part, self.right)
        self.left_b.wait_recv()
        part = out.at[rows(self.base + self.chunk(1) + h, h), self.cols]
        self.on_b = w.start(part, part, self.left)

    def gather_near(self):
        self.right_b.wait_recv()
        self.left_a.wait_recv()


ORDER = (2, 1, 3, 0)


class Flow:
    def __init__(self, q, wires, grads, out, bufs, tick, store):
        self.q, self.w, self.grads, self.out = q, wires, grads, out
        self.tick, self.store = tick, store
        acc, half, mid1, edge1, mid2, edge2, deep = bufs
        self.acc, self.half, self.deep = acc.at[q], half.at[q], deep.at[q]
        self.outer_bufs = mid1.at[q], edge1.at[q]
        self.inner_bufs = mid2.at[q], edge2.at[q]
        x, y, z, c = position()
        self.z, self.other = z, device(x, y, z, 1 - c)
        self.columns = [device(x, y, lax.rem(z + r, NZ), c) for r in range(1, NZ)]
        along_x = [x] + [device(lax.rem(x + s, NX), y, z, c) for s in (1, 3)]
        along_y = [y] + [device(x, lax.rem(y + s, NY), z, c) for s in (1, 3)]
        first, second = (along_x, along_y) if q % 2 == 0 else (along_y, along_x)
        self.outer, self.inner = Ring(wires, *first, 256), Ring(wires, *second, 64)
        place = (q % 2) * 256 + (q // 2) * LANES
        self.cols = pl.ds(pl.multiple_of(c * 512 + place, LANES), LANES)
        self.away = pl.ds(pl.multiple_of(512 - c * 512 + place, LANES), LANES)

    def swap(self):
        self.swaps = []
        for step in ORDER:
            here = rows(self.outer.chunk(step), 256)
            self.swaps.append(
                self.w.start(self.grads.at[here, self.away], self.half.at[here], self.other)
            )

    def back(self, start, size):
        part = self.out.at[rows(start, size), self.cols]
        self.backs.append(self.w.start(part, part, self.other))

    def steps(self):
        outer, inner, acc, z = self.outer, self.inner, self.acc, self.z
        for copy, step in zip(self.swaps, ORDER):
            here = rows(outer.chunk(step), 256)
            copy.wait_recv()
            acc[here, :] = self.grads[here, self.cols] + self.half[here, :]
            self.tick()
        outer.scatter_start(acc, 0, *self.outer_bufs)
        yield
        outer.scatter_mid()
        yield
        first = outer.scatter_end()
        inner.scatter_start(acc, first, *self.inner_bufs)
        yield
        inner.scatter_mid()
        yield
        second = inner.scatter_end()
        downs = []
        for r in range(1, NZ):
            part = acc.at[rows(second + lax.rem(z + r, NZ) * 8, 8)]
            downs.append(self.w.start(part, self.deep.at[r - 1], self.columns[r - 1]))
        yield
        for copy in downs:
            copy.wait_recv()
        here = rows(second + z * 8, 8)
        total = acc[here, :]
        for r in range(NZ - 1):
            total = total + self.deep[r]
        self.out[here, self.cols] = total
        part = self.out.at[here, self.cols]
        ups = [self.w.start(part, part, to) for to in self.columns]
        yield
        for copy in ups:
            copy.wait_recv()
        inner.gather_start(self.out, first, self.cols)
        yield
        inner.gather_mid()
        yield
        inner.gather_near()
        inner.on_a.wait_recv()
        inner.on_b.wait_recv()
        self.backs = []
        outer.gather_start(self.out, 0, self.cols)
        self.back(outer.chunk(0), 256)
        yield
        outer.gather_mid()
        yield
        outer.gather_near()
        self.back(outer.chunk(3), 256)
        self.back(outer.chunk(1), 256)
        yield
        outer.on_a.wait_recv()
        self.back(outer.chunk(2), 128)
        outer.on_b.wait_recv()
        self.back(outer.chunk(2) + 128, 128)
        self.store(self.cols)
        yield
        for copy in self.backs:
            copy.wait_recv()
        self.store(self.away)


def side_steps(wires, side, side_out, bufs):
    side0, side1, side2, side3 = bufs
    x, y, z, c = position()
    copy = wires.start(side, side0, device(x, y, z, 1 - c))
    yield
    copy.wait_recv()
    side1[x] = side[...] + side0[...]
    sides = [
        wires.start(side1.at[x], side1.at[x], device(lax.rem(x + r, NX), y, z, c))
        for r in range(1, NX)
    ]
    yield
    for copy in sides:
        copy.wait_recv()
    side2[y] = (side1[0] + side1[1]) + (side1[2] + side1[3])
    sides = [
        wires.start(side2.at[y], side2.at[y], device(x, lax.rem(y + r, NY), z, c))
        for r in range(1, NY)
    ]
    yield
    for copy in sides:
        copy.wait_recv()
    side3[z] = (side2[0] + side2[1]) + (side2[2] + side2[3])
    sides = [
        wires.start(side3.at[z], side3.at[z], device(x, y, lax.rem(z + r, NZ), c))
        for r in range(1, NZ)
    ]
    yield
    yield
    for copy in sides:
        copy.wait_recv()
    total = side3[0]
    for r in range(1, NZ):
        total = total + side3[r]
    side_out[...] = total


AR_BUFS = [
    pltpu.VMEM((FLOWS, 1024, LANES), F32),
    pltpu.VMEM((FLOWS, 1024, LANES), F32),
    pltpu.VMEM((FLOWS, 2, 128, LANES), F32),
    pltpu.VMEM((FLOWS, 2, 256, LANES), F32),
    pltpu.VMEM((FLOWS, 2, 32, LANES), F32),
    pltpu.VMEM((FLOWS, 2, 64, LANES), F32),
    pltpu.VMEM((FLOWS, 7, 8, LANES), F32),
    pltpu.VMEM((8, 256), F32),
    pltpu.VMEM((4, 8, 256), F32),
    pltpu.VMEM((4, 8, 256), F32),
    pltpu.VMEM((8, 8, 256), F32),
]


def greet(peers, sem):
    for peer in peers:
        pl.semaphore_signal(sem, inc=1, device_id=peer, device_id_type=MESH)


def owner_dp(group, forth=1):
    x, _, _, c = position()
    across = lax.rem(x + (NX + forth * (group // 2)), NX)
    return across * 2 + lax.rem(c + group % 2, 2)


class Exchange:
    def __init__(self, source, target, send, recv, forth):
        self.source, self.target, self.forth = source, target, forth
        self.send, self.recv, self.all = send, recv, []
        _, y, z, _ = position()
        self.y, self.z, self.me = y, z, y * NZ + z

    def start(self, group, begin=0, end=CODES):
        dp = owner_dp(group, self.forth)
        source, target = self.source.at[group], self.target.at[group]

        def copy(code, src, dst):
            return pltpu.make_async_remote_copy(
                src_ref=src,
                dst_ref=dst,
                send_sem=self.send.at[group],
                recv_sem=self.recv.at[group],
                device_id=(code, dp),
                device_id_type=MESH,
            )

        def one(i, carry):
            code = lax.rem(self.y + lax.div(i, NZ), NY) * NZ + lax.rem(self.z + lax.rem(i, NZ), NZ)
            copy(code, source.at[code], target.at[self.me]).start()
            return carry

        own = 1 if group == 0 else 0
        lax.fori_loop(max(own, begin), end, one, 0)
        if begin:
            return
        if own:
            self.target[group, self.me] = self.source[group, self.me]
        whole = pl.ds(0, CODES - own)
        near = self.y * NZ + lax.rem(self.z + 1, NZ)
        self.all.append(copy(near, source.at[whole], target.at[whole]))

    def arrived(self, group):
        self.all[group].wait_recv()

    def drain(self):
        for copy in self.all:
            copy.wait_send()


def dot(a, b):
    return jnp.dot(a, b, preferred_element_type=F32)


def halves(value):
    high = value.astype(BF16)
    low = (value - high.astype(F32)).astype(BF16)
    return jnp.concatenate([high, low], axis=1)


def joined(value):
    return value[:, :256] + value[:, 256:]


def upright(row):
    return jnp.transpose(jnp.broadcast_to(row, (128, row.shape[1])))


def iota(shape, dim):
    return lax.broadcasted_iota(jnp.int32, shape, dim)


def one_hot(condition):
    return jnp.where(condition, 1.0, 0.0).astype(BF16)


def slots_of(group, shape, dim):
    place = iota(shape, dim)
    slot = (place // CAP) * (GROUPS * CAP) + place % CAP + owner_dp(group) * CAP
    return slot.astype(F32)


def whole_kernel(
    codebook_h, weight_in_h, bias_in, weight_out_h, bias_out, latents_h, cotangent_h, owner, code,
    latent_grad_h, out_h, side_out,
    codebook, weight_in, weight_out, latents, cotangent, slot_col, values, send_a, recv_a, send_b,
    recv_b, ids_out, ids_in, slope, hidden_t, codebook_t, weight_out_t, projected, base, picks,
    code_low, grads, side, latent_grad, out,
    load, keep, ids_s, ids_r, a_s, a_r, b_s, b_r, near_a, near_b, wire_s, wire_r, *bufs,
):
    x, y, z, c = position()
    pairs = (
        (latents_h, latents), (cotangent_h, cotangent), (codebook_h, codebook),
        (weight_in_h, weight_in), (weight_out_h, weight_out),
    )
    loads = [pltpu.make_async_copy(src, dst, load.at[i]) for i, (src, dst) in enumerate(pairs)]
    for copy in loads:
        copy.start()
    barrier = pltpu.get_barrier_semaphore()
    row_peers = [
        device(lax.rem(x + r, NX), y, z, lax.rem(c + s, 2))
        for r in range(NX) for s in range(2) if r + s
    ]
    y_peers = [device(x, lax.rem(y + r, NY), z, c) for r in range(1, NY)]
    z_peers = [device(x, y, lax.rem(z + r, NZ), c) for r in range(1, NZ)]
    line_peers = row_peers + y_peers + z_peers
    greet(line_peers, barrier)

    owner_row = owner[...].astype(F32)
    code_row = code[...].astype(F32) + 1.0
    owner_col = upright(owner_row)
    lower = iota((128, 128), 0) < iota((128, 128), 1)
    ranks = []
    for i in range(8):
        name = owner_row[:, 128 * i : 128 * i + 128]
        count = jnp.where((owner_col[128 * i : 128 * i + 128] == name) & lower, 1.0, 0.0)
        for j in range(i):
            count += jnp.where(owner_col[128 * j : 128 * j + 128] == name, 1.0, 0.0)
        ranks.append(jnp.sum(count, axis=0, keepdims=True))
    rank_row = jnp.concatenate(ranks, axis=1)
    slot_row = owner_row * CAP + rank_row
    slot_col[...] = upright(slot_row)
    pl.semaphore_wait(barrier, len(line_peers))
    greet(row_peers, near_a)

    rank_col = upright(rank_row)
    code_col = upright(code_row)
    code_high = jnp.floor(code_col * (1.0 / 32))
    mine = rank_col == iota((1024, 128), 1).astype(F32)
    digits = jnp.concatenate(
        [
            jnp.where(mine, code_high, 0.0).astype(BF16),
            jnp.where(mine, code_col - 32.0 * code_high, 0.0).astype(BF16),
        ],
        axis=1,
    )
    place = iota((256, 1024), 0)
    group = place // CODES
    across = (x + group // 2) % NX * 2 + (c + group % 2) % 2
    named = dot(one_hot(owner_row == ((place % CODES) * GROUPS + across).astype(F32)), digits)
    named = named[:, :128] * 32.0 + named[:, 128:] - 1.0
    ids_out[...] = named.reshape(GROUPS, CODES, 1, 128)
    loads[0].wait()
    loads[1].wait()
    values[pl.ds(0, 1024), :] = halves(cotangent[...] - latents[...])
    pl.semaphore_wait(near_a, len(row_peers))
    greet(y_peers, near_b)

    names = Exchange(ids_out, ids_in, ids_s, ids_r, 1)
    forth = Exchange(send_a, recv_a, a_s, a_r, 1)
    answers = Exchange(send_b, recv_b, b_s, b_r, -1)
    for b in range(GROUPS):
        hot = one_hot(slot_row == slots_of(b, (256, 1024), 0))
        block = joined(dot(hot, values[pl.ds(0, 1024), :]))
        send_a[b] = block.reshape(CODES, CAP, 256)
        if b == 0:
            pl.semaphore_wait(near_b, len(y_peers))
            for k in range(GROUPS):
                names.start(k)
        forth.start(b)

    for copy in loads[2:]:
        copy.wait()
    weight_out_t[...] = jnp.transpose(weight_out[...].astype(F32)).astype(BF16)

    def forward(i, carry):
        here = rows(i * 256, 256)
        block = codebook[here, :]
        pre = dot(block, weight_in[...]) + bias_in[...]
        tangent = jnp.tanh(scale_gelu * (pre + cubic_term * pre * pre * pre))
        value = 0.5 * pre * (1.0 + tangent)
        slope[here, :] = 0.5 * (1.0 + tangent) + 0.5 * pre * (
            1.0 - tangent * tangent
        ) * scale_gelu * (1.0 + 3.0 * cubic_term * pre * pre)
        hidden = value.astype(BF16)
        cols = pl.ds(pl.multiple_of(i * 256, 256), 256)
        hidden_t[:, cols] = jnp.transpose(value).astype(BF16)
        codebook_t[:, cols] = jnp.transpose(block.astype(F32)).astype(BF16)
        block = dot(hidden, weight_out[...]) + bias_out[...]
        base[here, :] = block
        projected[here, :] = halves(block)
        return carry

    lax.fori_loop(0, 4, forward, 0)

    for b in range(GROUPS):
        names.arrived(b)
    ones = jnp.ones((256, 128), BF16)
    own = iota((256, 128), 0) % CAP == iota((256, 128), 1)
    for b in range(GROUPS):
        ids = ids_in[b]
        ids = jnp.broadcast_to(ids, (CODES, CAP, 128)).reshape(256, 128)
        ids = jnp.where(own, ids, 0.0)
        ids_col = jnp.sum(ids, axis=1, keepdims=True)
        ids_row = jnp.sum(jnp.transpose(ids), axis=0, keepdims=True)
        hot = one_hot(ids_col == iota((256, 1024), 1).astype(F32))
        send_b[b] = joined(dot(hot, projected[...])).reshape(CODES, CAP, 256)
        for i in range(4):
            hot = one_hot(ids_row == (iota((256, 256), 0) + 256 * i).astype(F32))
            picks[b, pl.ds(i * 256, 256), :] = hot
    for i in range(4):
        here = pl.ds(i * 256, 256)
        count = dot(picks[0, here, :], ones)
        for j in range(1, GROUPS):
            count += dot(picks[j, here, :], ones)
        base[here, :] = base[here, :] * jnp.concatenate([count, count], axis=1)

    for b in range(GROUPS):
        forth.arrived(b)
        if b == GROUPS - 1:
            answers.start(0)
        part = halves(recv_a[b].reshape(256, 256))
        for i in range(4):
            here = pl.ds(i * 256, 256)
            base[here, :] = base[here, :] + joined(dot(picks[b, here, :], part))
    code_low[...] = base[...].astype(BF16)
    side[...] = jnp.zeros((8, 256), F32)
    side[4:5, :] = jnp.sum(base[...], axis=0, keepdims=True)

    def gradient(b):
        cols = pl.ds(pl.multiple_of(b * 256, 256), 256)
        back = dot(code_low[...], weight_out_t[:, cols])
        low = (back * slope[:, cols]).astype(BF16)
        side[pl.ds(b, 1), :] = jnp.sum(low.astype(F32), axis=0, keepdims=True)
        grads[pl.ds(0, 768), cols] = dot(codebook_t[...], low)
        grads[pl.ds(768, 256), cols] = dot(hidden_t[rows(b * 256, 256), :], code_low[...])

    wires = Wires(wire_s, wire_r)
    chunks = [(k, i) for k in range(1, GROUPS) for i in range(0, CODES, PACE)]
    kept = []

    def tick():
        if chunks:
            k, i = chunks.pop(0)
            answers.start(k, i, i + PACE)

    def store(cols):
        copy = pltpu.make_async_copy(out.at[:, cols], out_h.at[:, cols], keep.at[len(kept)])
        copy.start()
        kept.append(copy)

    flows = [Flow(q, wires, grads, out, bufs[:7], tick, store) for q in range(FLOWS)]
    for q in range(2):
        gradient(2 - 2 * c + q)
    for flow in flows:
        flow.swap()
    for q in range(2):
        gradient(2 * c + q)

    def chosen(b):
        answers.arrived(b)
        part = halves(recv_b[b].reshape(256, 256))
        for i in range(4):
            here = pl.ds(i * 256, 256)
            slot, place = slot_col[here, :], slots_of(b, (256, 256), 1)
            hot = jnp.concatenate(
                [one_hot(slot == place[:, k * 128 : k * 128 + 128]) for k in range(2)], axis=1
            )
            total = joined(dot(hot, part))
            if b:
                total = total + latent_grad[here, :]
            if b == GROUPS - 1:
                total = cotangent[here, :] - 0.25 * (total - latents[here, :])
            latent_grad[here, :] = total

    picked = {11: [0], 12: [1], 13: [2], 14: [3], 15: [4], 16: [5], 17: [6], 18: [7]}
    running = []
    waiting = [side_steps(wires, side, side_out, bufs[7:])] + [flow.steps() for flow in flows]
    joins = {0: 3, 2: 2}
    turn = 0
    while running or waiting or turn <= max(picked):
        for _ in range(joins.get(turn, 0)):
            running.append(waiting.pop(0))
        for flow in list(running):
            if next(flow, flow) is flow:
                running.remove(flow)
            tick()
        for b in picked.get(turn, []):
            while chunks and chunks[0][0] <= b:
                tick()
            chosen(b)
        turn += 1
    copy = pltpu.make_async_copy(latent_grad, latent_grad_h, keep.at[len(kept)])
    copy.start()
    for copy in kept + [copy]:
        copy.wait()
    wires.drain()
    for exchange in (names, forth, answers):
        exchange.drain()
    assert wires.used == AR_WIRES, wires.used


def whole(codebook, weight_in, bias_in, weight_out, bias_out, latents, cotangent, owner, code):
    vmem, anywhere = (pl.BlockSpec(memory_space=m) for m in (pltpu.VMEM, pl.ANY))
    dma, plain = pltpu.SemaphoreType.DMA, pltpu.SemaphoreType.REGULAR
    scratch = [
        pltpu.VMEM((1024, 768), BF16),
        pltpu.VMEM((768, 1024), BF16),
        pltpu.VMEM((1024, 256), BF16),
        pltpu.VMEM((1024, 256), F32),
        pltpu.VMEM((1024, 256), F32),
        pltpu.VMEM((1024, 128), F32),
        pltpu.VMEM((1024, 512), BF16),
    ]
    scratch += [pltpu.VMEM((GROUPS, CODES, CAP, 256), F32)] * 4
    scratch += [pltpu.VMEM((GROUPS, CODES, 1, 128), F32)] * 2
    scratch += [
        pltpu.VMEM((1024, 1024), F32),
        pltpu.VMEM((1024, 1024), BF16),
        pltpu.VMEM((768, 1024), BF16),
        pltpu.VMEM((256, 1024), BF16),
        pltpu.VMEM((1024, 512), BF16),
        pltpu.VMEM((1024, 256), F32),
        pltpu.VMEM((GROUPS, 1024, 256), BF16),
        pltpu.VMEM((1024, 256), BF16),
        pltpu.VMEM((1024, 1024), F32),
        pltpu.VMEM((8, 256), F32),
        pltpu.VMEM((1024, 256), F32),
        pltpu.VMEM((1024, 1024), F32),
        dma((5,)),
        dma((2 * FLOWS + 1,)),
        *[dma((GROUPS,))] * 6,
        plain, plain,
        dma((AR_WIRES,)), dma((AR_WIRES,)),
    ]
    return pl.pallas_call(
        whole_kernel,
        out_shape=(
            jax.ShapeDtypeStruct((1024, 256), F32),
            jax.ShapeDtypeStruct((1024, 1024), F32),
            jax.ShapeDtypeStruct((8, 256), F32),
        ),
        in_specs=[anywhere, anywhere, vmem, anywhere, vmem, anywhere, anywhere, vmem, vmem],
        out_specs=(anywhere, anywhere, vmem),
        scratch_shapes=scratch + AR_BUFS,
        compiler_params=pltpu.CompilerParams(
            collective_id=1, has_side_effects=True, vmem_limit_bytes=60 * 2**20
        ),
    )(codebook, weight_in, bias_in, weight_out, bias_out, latents, cotangent, owner, code)


def finish_kernel(latent_grad, grads, side, latent_out, in_out, bias_in_out, w_out, bias_out, *bufs):
    part, whole_part, gets, puts = bufs
    pieces = []
    for j in range(2):
        here = pl.ds(j * 512, 512)
        pieces.append((latent_grad.at[here], part.at[here], [(part.at[here], latent_out.at[here])]))
    for j in range(6):
        here = pl.ds(j * 128, 128)
        pieces.append((grads.at[here], whole_part.at[here], [(whole_part.at[here], in_out.at[here])]))
    here = pl.ds(768, 256)
    pairs = [
        (whole_part.at[here, pl.ds(j * 256, 256)], w_out.at[pl.ds(j * 256, 256)]) for j in range(4)
    ]
    pieces.append((grads.at[here], whole_part.at[here], pairs))
    reads = [pltpu.make_async_copy(a, b, gets.at[i]) for i, (a, b, _) in enumerate(pieces)]
    for copy in reads:
        copy.start()
    for j in range(4):
        bias_in_out[:, j * 256 : j * 256 + 256] = side[j : j + 1, :]
    bias_out[...] = side[4:5, :]
    writes = []
    for copy, (_, _, pairs) in zip(reads, pieces):
        copy.wait()
        for a, b in pairs:
            writes.append(pltpu.make_async_copy(a, b, puts.at[len(writes)]))
            writes[-1].start()
    for copy in writes:
        copy.wait()


def finish(latent_grad, grads, side):
    vmem, anywhere = (pl.BlockSpec(memory_space=m) for m in (pltpu.VMEM, pl.ANY))
    return pl.pallas_call(
        finish_kernel,
        out_shape=tuple(
            jax.ShapeDtypeStruct(shape, F32)
            for shape in ((1024, 256), (768, 1024), (1, 1024), (1024, 256), (1, 256))
        ),
        in_specs=[anywhere, anywhere, vmem],
        out_specs=(anywhere, anywhere, vmem, anywhere, vmem),
        scratch_shapes=[
            pltpu.VMEM((1024, 256), F32),
            pltpu.VMEM((1024, 1024), F32),
            pltpu.SemaphoreType.DMA((9,)),
            pltpu.SemaphoreType.DMA((12,)),
        ],
        compiler_params=pltpu.CompilerParams(vmem_limit_bytes=60 * 2**20),
    )(latent_grad, grads, side)


def per_device(
    codebook, weight_in, bias_in, weight_out, bias_out, latents, cotangent, code_owner, code_row
):
    parts = whole(
        codebook, weight_in, bias_in[None], weight_out, bias_out[None], latents, cotangent,
        code_owner.reshape(1, 1024), code_row.reshape(1, 1024),
    )
    latent_grad, gw_in, gb_in, gw_out, gb_out = finish(*parts)
    return (latent_grad, gw_in, gb_in[0], gw_out, gb_out[0])


def solution(mesh):
    placed = (
        P(("code", "dp"), None),
        P(),
        P(),
        P(),
        P(),
        P(("code", "dp"), None),
        P(("code", "dp"), None),
        P(("code", "dp"), None),
        P(("code", "dp")),
    )
    return jax.shard_map(
        per_device,
        mesh=mesh,
        in_specs=placed,
        out_specs=(P(("code", "dp"), None), P(), P(), P(), P()),
        check_vma=False,
    )
```

```python
import jax
import jax.numpy as jnp
from jax import lax
from jax.experimental import pallas as pl
from jax.experimental.pallas import tpu as pltpu
from jax.sharding import PartitionSpec as P

scale_gelu = 0.7978845608028654
cubic_term = 0.044715


MESH = pl.DeviceIdType.MESH
NX, NY, NZ = 4, 4, 8
CAP, DEVICES, GROUPS, CODES = 8, 256, 8, 32
PACE = 4
LANES = 256
F32, BF16 = jnp.float32, jnp.bfloat16


def rows(start, size):
    return pl.ds(pl.multiple_of(start, 8), size)


class Wires:
    def __init__(self, send, recv):
        self.send, self.recv, self.used, self.open = send, recv, 0, []

    def start(self, src, dst, to):
        k = self.used
        self.used += 1
        copy = pltpu.make_async_remote_copy(
            src_ref=src,
            dst_ref=dst,
            send_sem=self.send.at[k],
            recv_sem=self.recv.at[k],
            device_id=to,
            device_id_type=MESH,
        )
        copy.start()
        self.open.append(copy)
        return copy

    def drain(self):
        for copy in self.open:
            copy.wait_send()


FLOWS = 512 // LANES
AR_WIRES = FLOWS * (4 + 6 + 3 + 7 + 7 + 3 + 6 + 5) + 14


def position():
    code, dp = lax.axis_index("code"), lax.axis_index("dp")
    return lax.div(dp, 2), lax.div(code, NZ), lax.rem(code, NZ), lax.rem(dp, 2)


def device(x, y, z, c):
    return (y * NZ + z, x * 2 + c)


class Ring:
    def __init__(self, wires, spot, right, left, size):
        self.w, self.p, self.n = wires, spot, size
        self.right, self.left = right, left
        self.h = size // 2

    def chunk(self, step):
        return lax.rem(self.p + step, 4) * self.n

    def scatter_start(self, acc, base, mid, edge):
        n, h, w = self.n, self.h, self.w
        self.acc, self.base, self.mid, self.edge = acc, base, mid, edge
        far, nxt, prv = (base + self.chunk(s) for s in (2, 1, 3))
        self.nxt, self.prv = nxt, prv
        self.far_a = w.start(acc.at[rows(far, h)], mid.at[0], self.right)
        self.far_b = w.start(acc.at[rows(far + h, h)], mid.at[1], self.left)
        self.near_b = w.start(acc.at[rows(nxt + h, h)], edge.at[0, pl.ds(h, h)], self.right)
        self.near_a = w.start(acc.at[rows(prv, h)], edge.at[1, pl.ds(0, h)], self.left)

    def scatter_mid(self):
        h, w, acc = self.h, self.w, self.acc
        self.far_a.wait_recv()
        here = rows(self.nxt, h)
        acc[here, :] = acc[here, :] + self.mid[0]
        self.pass_a = w.start(acc.at[here], self.edge.at[0, pl.ds(0, h)], self.right)
        self.far_b.wait_recv()
        here = rows(self.prv + h, h)
        acc[here, :] = acc[here, :] + self.mid[1]
        self.pass_b = w.start(acc.at[here], self.edge.at[1, pl.ds(h, h)], self.left)

    def scatter_end(self):
        for copy in (self.near_b, self.near_a, self.pass_a, self.pass_b):
            copy.wait_recv()
        mine = self.base + self.chunk(0)
        here = rows(mine, self.n)
        self.acc[here, :] = self.acc[here, :] + (self.edge[0] + self.edge[1])
        return mine

    def gather_start(self, out, base, cols):
        h, w = self.h, self.w
        self.out, self.base, self.cols = out, base, cols
        mine = base + self.chunk(0)
        first, second = (out.at[rows(mine + s, h), cols] for s in (0, h))
        self.right_a = w.start(first, first, self.right)
        self.left_b = w.start(second, second, self.left)
        self.right_b = w.start(second, second, self.right)
        self.left_a = w.start(first, first, self.left)

    def gather_mid(self):
        h, w, out = self.h, self.w, self.out
        self.right_a.wait_recv()
        part = out.at[rows(self.base + self.chunk(3), h), self.cols]
        self.on_a = w.start(part, part, self.right)
        self.left_b.wait_recv()
        part = out.at[rows(self.base + self.chunk(1) + h, h), self.cols]
        self.on_b = w.start(part, part, self.left)

    def gather_near(self):
        self.right_b.wait_recv()
        self.left_a.wait_recv()


class Direct:
    def __init__(self, wires, spot, peers, size):
        self.w, self.p, self.peers, self.n = wires, spot, peers, size

    def chunk(self, step):
        return lax.rem(self.p + step, 4) * self.n

    def scatter_start(self, acc, base, edge):
        self.acc, self.base, self.edge = acc, base, edge
        self.copies = [
            self.w.start(acc.at[rows(base + self.chunk(r), self.n)], edge.at[r - 1], to)
            for r, to in zip((1, 2, 3), self.peers)
        ]

    def scatter_end(self):
        for copy in self.copies:
            copy.wait_recv()
        mine = self.base + self.chunk(0)
        here = rows(mine, self.n)
        total = (self.edge[0] + self.edge[1]) + self.edge[2]
        self.acc[here, :] = self.acc[here, :] + total
        return mine

    def gather_start(self, out, base, cols):
        part = out.at[rows(base + self.chunk(0), self.n), cols]
        self.copies = [self.w.start(part, part, to) for to in self.peers]

    def gather_end(self):
        for copy in self.copies:
            copy.wait_recv()


ORDER = (2, 1, 3, 0)


class Flow:
    def __init__(self, q, wires, grads, out, bufs, tick):
        self.q, self.w, self.grads, self.out = q, wires, grads, out
        self.tick = tick
        acc, half, mid1, edge1, edge2, deep = bufs
        self.acc, self.half, self.deep = acc.at[q], half.at[q], deep.at[q]
        self.outer_bufs = mid1.at[q], edge1.at[q]
        self.inner_buf = edge2.at[q]
        x, y, z, c = position()
        self.z, self.other = z, device(x, y, z, 1 - c)
        self.columns = [device(x, y, lax.rem(z + r, NZ), c) for r in range(1, NZ)]
        along_x = x, [device(lax.rem(x + s, NX), y, z, c) for s in (1, 2, 3)]
        along_y = y, [device(x, lax.rem(y + s, NY), z, c) for s in (1, 2, 3)]
        first, second = (along_x, along_y) if q % 2 == 0 else (along_y, along_x)
        self.outer = Ring(wires, first[0], first[1][0], first[1][2], 256)
        self.inner = Direct(wires, *second, 64)
        place = (q % 2) * 256 + (q // 2) * LANES
        self.cols = pl.ds(pl.multiple_of(c * 512 + place, LANES), LANES)
        self.away = pl.ds(pl.multiple_of(512 - c * 512 + place, LANES), LANES)

    def swap(self):
        self.swaps = []
        for step in ORDER:
            here = rows(self.outer.chunk(step), 256)
            self.swaps.append(
                self.w.start(self.grads.at[here, self.away], self.half.at[here], self.other)
            )

    def back(self, start, size):
        part = self.out.at[rows(start, size), self.cols]
        self.backs.append(self.w.start(part, part, self.other))

    def steps(self):
        outer, inner, acc, z = self.outer, self.inner, self.acc, self.z
        for copy, step in zip(self.swaps, ORDER):
            here = rows(outer.chunk(step), 256)
            copy.wait_recv()
            acc[here, :] = self.grads[here, self.cols] + self.half[here, :]
            self.tick()
        outer.scatter_start(acc, 0, *self.outer_bufs)
        yield
        outer.scatter_mid()
        yield
        first = outer.scatter_end()
        inner.scatter_start(acc, first, self.inner_buf)
        yield
        second = inner.scatter_end()
        downs = []
        for r in range(1, NZ):
            part = acc.at[rows(second + lax.rem(z + r, NZ) * 8, 8)]
            downs.append(self.w.start(part, self.deep.at[r - 1], self.columns[r - 1]))
        yield
        for copy in downs:
            copy.wait_recv()
        here = rows(second + z * 8, 8)
        total = acc[here, :]
        for r in range(NZ - 1):
            total = total + self.deep[r]
        self.out[here, self.cols] = total
        part = self.out.at[here, self.cols]
        ups = [self.w.start(part, part, to) for to in self.columns]
        yield
        for copy in ups:
            copy.wait_recv()
        inner.gather_start(self.out, first, self.cols)
        yield
        inner.gather_end()
        self.backs = []
        outer.gather_start(self.out, 0, self.cols)
        self.back(outer.chunk(0), 256)
        yield
        outer.gather_mid()
        yield
        outer.gather_near()
        self.back(outer.chunk(3), 256)
        self.back(outer.chunk(1), 256)
        yield
        outer.on_a.wait_recv()
        self.back(outer.chunk(2), 128)
        outer.on_b.wait_recv()
        self.back(outer.chunk(2) + 128, 128)
        yield
        for copy in self.backs:
            copy.wait_recv()


def side_steps(wires, side, side_out, bufs):
    side0, side1, side2, side3 = bufs
    x, y, z, c = position()
    copy = wires.start(side, side0, device(x, y, z, 1 - c))
    yield
    copy.wait_recv()
    side1[x] = side[...] + side0[...]
    sides = [
        wires.start(side1.at[x], side1.at[x], device(lax.rem(x + r, NX), y, z, c))
        for r in range(1, NX)
    ]
    yield
    for copy in sides:
        copy.wait_recv()
    side2[y] = (side1[0] + side1[1]) + (side1[2] + side1[3])
    sides = [
        wires.start(side2.at[y], side2.at[y], device(x, lax.rem(y + r, NY), z, c))
        for r in range(1, NY)
    ]
    yield
    for copy in sides:
        copy.wait_recv()
    side3[z] = (side2[0] + side2[1]) + (side2[2] + side2[3])
    sides = [
        wires.start(side3.at[z], side3.at[z], device(x, y, lax.rem(z + r, NZ), c))
        for r in range(1, NZ)
    ]
    yield
    yield
    for copy in sides:
        copy.wait_recv()
    total = side3[0]
    for r in range(1, NZ):
        total = total + side3[r]
    side_out[...] = total


AR_BUFS = [
    pltpu.VMEM((FLOWS, 1024, LANES), F32),
    pltpu.VMEM((FLOWS, 1024, LANES), F32),
    pltpu.VMEM((FLOWS, 2, 128, LANES), F32),
    pltpu.VMEM((FLOWS, 2, 256, LANES), F32),
    pltpu.VMEM((FLOWS, 3, 64, LANES), F32),
    pltpu.VMEM((FLOWS, 7, 8, LANES), F32),
    pltpu.VMEM((8, 256), F32),
    pltpu.VMEM((4, 8, 256), F32),
    pltpu.VMEM((4, 8, 256), F32),
    pltpu.VMEM((8, 8, 256), F32),
]


def greet(peers, sem):
    for peer in peers:
        pl.semaphore_signal(sem, inc=1, device_id=peer, device_id_type=MESH)


def owner_dp(group, forth=1):
    x, _, _, c = position()
    across = lax.rem(x + (NX + forth * (group // 2)), NX)
    return across * 2 + lax.rem(c + group % 2, 2)


class Exchange:
    def __init__(self, source, target, send, recv, forth):
        self.source, self.target, self.forth = source, target, forth
        self.send, self.recv, self.all = send, recv, []
        _, y, z, _ = position()
        self.y, self.z, self.me = y, z, y * NZ + z

    def start(self, group, begin=0, end=CODES):
        dp = owner_dp(group, self.forth)
        source, target = self.source.at[group], self.target.at[group]

        def copy(code, src, dst):
            return pltpu.make_async_remote_copy(
                src_ref=src,
                dst_ref=dst,
                send_sem=self.send.at[group],
                recv_sem=self.recv.at[group],
                device_id=(code, dp),
                device_id_type=MESH,
            )

        def one(i, carry):
            code = lax.rem(self.y + lax.div(i, NZ), NY) * NZ + lax.rem(self.z + lax.rem(i, NZ), NZ)
            copy(code, source.at[code], target.at[self.me]).start()
            return carry

        own = 1 if group == 0 else 0
        lax.fori_loop(max(own, begin), end, one, 0)
        if begin:
            return
        if own:
            self.target[group, self.me] = self.source[group, self.me]
        whole = pl.ds(0, CODES - own)
        near = self.y * NZ + lax.rem(self.z + 1, NZ)
        self.all.append(copy(near, source.at[whole], target.at[whole]))

    def arrived(self, group):
        self.all[group].wait_recv()

    def drain(self):
        for copy in self.all:
            copy.wait_send()


def dot(a, b):
    return jnp.dot(a, b, preferred_element_type=F32)


def halves(value):
    high = value.astype(BF16)
    low = (value - high.astype(F32)).astype(BF16)
    return jnp.concatenate([high, low], axis=1)


def joined(value):
    return value[:, :256] + value[:, 256:]


def upright(row):
    return jnp.transpose(jnp.broadcast_to(row, (128, row.shape[1])))


def iota(shape, dim):
    return lax.broadcasted_iota(jnp.int32, shape, dim)


def one_hot(condition):
    return jnp.where(condition, 1.0, 0.0).astype(BF16)


def slots_of(group, shape, dim):
    place = iota(shape, dim)
    slot = (place // CAP) * (GROUPS * CAP) + place % CAP + owner_dp(group) * CAP
    return slot.astype(F32)


def whole_kernel(
    codebook_h, weight_in_h, bias_in, weight_out_h, bias_out, latents_h, cotangent_h, owner, code,
    latent_grad, out, side_out,
    codebook, weight_in, weight_out, latents, cotangent, slot_col, values, send_a, recv_a, send_b,
    recv_b, ids_out, ids_mid, ids_sum, ids_in, slope, hidden_t, codebook_t, weight_out_t, projected, base, picks,
    code_low, grads, side,
    load, ids_s, ids_r, c_s, c_r, a_s, a_r, b_s, b_r, near_a, near_b, wire_s, wire_r, *bufs,
):
    x, y, z, c = position()
    pairs = (
        (latents_h, latents), (cotangent_h, cotangent), (codebook_h, codebook),
        (weight_in_h, weight_in), (weight_out_h, weight_out),
    )
    loads = [pltpu.make_async_copy(src, dst, load.at[i]) for i, (src, dst) in enumerate(pairs)]
    for copy in loads:
        copy.start()
    barrier = pltpu.get_barrier_semaphore()
    row_peers = [
        device(lax.rem(x + r, NX), y, z, lax.rem(c + s, 2))
        for r in range(NX) for s in range(2) if r + s
    ]
    y_peers = [device(x, lax.rem(y + r, NY), z, c) for r in range(1, NY)]
    z_peers = [device(x, y, lax.rem(z + r, NZ), c) for r in range(1, NZ)]
    line_peers = row_peers + y_peers + z_peers
    greet(line_peers, barrier)

    owner_row = owner[...].astype(F32)
    code_row = code[...].astype(F32) + 1.0
    owner_col = upright(owner_row)
    lower = iota((128, 128), 0) < iota((128, 128), 1)
    ranks = []
    for i in range(8):
        name = owner_row[:, 128 * i : 128 * i + 128]
        count = jnp.where((owner_col[128 * i : 128 * i + 128] == name) & lower, 1.0, 0.0)
        for j in range(i):
            count += jnp.where(owner_col[128 * j : 128 * j + 128] == name, 1.0, 0.0)
        ranks.append(jnp.sum(count, axis=0, keepdims=True))
    rank_row = jnp.concatenate(ranks, axis=1)
    slot_row = owner_row * CAP + rank_row
    slot_col[...] = upright(slot_row)
    pl.semaphore_wait(barrier, len(line_peers))
    greet(y_peers, near_a)

    rank_col = upright(rank_row)
    code_col = upright(code_row)
    code_high = jnp.floor(code_col * (1.0 / 32))
    lane = iota((1024, 128), 1)
    mine = (rank_col == (lane % CAP).astype(F32)) & (lane < GROUPS * CAP)
    digits = jnp.concatenate(
        [
            jnp.where(mine, code_high, 0.0).astype(BF16),
            jnp.where(mine, code_col - 32.0 * code_high, 0.0).astype(BF16),
        ],
        axis=1,
    )
    place = iota((256, 1024), 0)
    group = place // CODES
    across = (x + group // 2) % NX * 2 + (c + group % 2) % 2
    named = dot(one_hot(owner_row == ((place % CODES) * GROUPS + across).astype(F32)), digits)
    named = named[:, :128] * 32.0 + named[:, 128:]
    ours = iota((256, 128), 1) // CAP == iota((256, 128), 0) // CODES
    ids_out[...] = jnp.where(ours, named, 0.0).reshape(GROUPS, CODES, 1, 128)
    aside = []
    for b in range(1, GROUPS):
        aside.append(
            pltpu.make_async_remote_copy(
                src_ref=ids_out.at[b],
                dst_ref=ids_mid.at[b],
                send_sem=ids_s.at[b],
                recv_sem=ids_r.at[b],
                device_id=(y * NZ + z, owner_dp(b)),
                device_id_type=MESH,
            )
        )
        aside[-1].start()
    loads[0].wait()
    loads[1].wait()
    values[pl.ds(0, 1024), :] = halves(cotangent[...] - latents[...])
    pl.semaphore_wait(near_a, len(y_peers))
    greet(row_peers, near_b)

    names = Exchange(ids_sum, ids_in, c_s, c_r, 1)
    forth = Exchange(send_a, recv_a, a_s, a_r, 1)
    answers = Exchange(send_b, recv_b, b_s, b_r, -1)
    for b in range(GROUPS):
        hot = one_hot(slot_row == slots_of(b, (256, 1024), 0))
        block = joined(dot(hot, values[pl.ds(0, 1024), :]))
        send_a[b] = block.reshape(CODES, CAP, 256)
        if b == 1:
            pl.semaphore_wait(near_b, len(row_peers))
        forth.start(b)
        if b == 1:
            total = ids_out[0]
            for k in range(1, GROUPS):
                aside[k - 1].wait_recv()
                total = total + ids_mid[k]
            ids_sum[0] = total
            names.start(0)

    for copy in loads[2:]:
        copy.wait()
    weight_out_t[...] = jnp.transpose(weight_out[...].astype(F32)).astype(BF16)

    def forward(i, carry):
        here = rows(i * 256, 256)
        block = codebook[here, :]
        pre = dot(block, weight_in[...]) + bias_in[...]
        tangent = jnp.tanh(scale_gelu * (pre + cubic_term * pre * pre * pre))
        value = 0.5 * pre * (1.0 + tangent)
        slope[here, :] = 0.5 * (1.0 + tangent) + 0.5 * pre * (
            1.0 - tangent * tangent
        ) * scale_gelu * (1.0 + 3.0 * cubic_term * pre * pre)
        hidden = value.astype(BF16)
        cols = pl.ds(pl.multiple_of(i * 256, 256), 256)
        hidden_t[:, cols] = jnp.transpose(value).astype(BF16)
        codebook_t[:, cols] = jnp.transpose(block.astype(F32)).astype(BF16)
        block = dot(hidden, weight_out[...]) + bias_out[...]
        base[here, :] = block
        projected[here, :] = halves(block)
        return carry

    lax.fori_loop(0, 4, forward, 0)

    names.arrived(0)
    ones = jnp.ones((256, 128), BF16)
    for b in range(GROUPS):
        ids = ids_in[0]
        own = iota((256, 128), 0) % CAP + b * CAP == iota((256, 128), 1)
        ids = jnp.broadcast_to(ids, (CODES, CAP, 128)).reshape(256, 128)
        ids = jnp.where(own, ids, 0.0)
        ids_col = jnp.sum(ids, axis=1, keepdims=True)
        ids_row = jnp.sum(jnp.transpose(ids), axis=0, keepdims=True)
        hot = one_hot(ids_col == (iota((256, 1024), 1) + 1).astype(F32))
        send_b[b] = joined(dot(hot, projected[...])).reshape(CODES, CAP, 256)
        for i in range(4):
            hot = one_hot(ids_row == (iota((256, 256), 0) + (256 * i + 1)).astype(F32))
            picks[b, pl.ds(i * 256, 256), :] = hot
    for i in range(4):
        here = pl.ds(i * 256, 256)
        count = dot(picks[0, here, :], ones)
        for j in range(1, GROUPS):
            count += dot(picks[j, here, :], ones)
        base[here, :] = base[here, :] * jnp.concatenate([count, count], axis=1)

    for b in range(GROUPS):
        forth.arrived(b)
        if b == GROUPS - 1:
            answers.start(0)
        part = halves(recv_a[b].reshape(256, 256))
        for i in range(4):
            here = pl.ds(i * 256, 256)
            base[here, :] = base[here, :] + joined(dot(picks[b, here, :], part))
    code_low[...] = base[...].astype(BF16)
    side[...] = jnp.zeros((8, 256), F32)
    side[4:5, :] = jnp.sum(base[...], axis=0, keepdims=True)

    def gradient(b):
        cols = pl.ds(pl.multiple_of(b * 256, 256), 256)
        back = dot(code_low[...], weight_out_t[:, cols])
        low = (back * slope[:, cols]).astype(BF16)
        side[pl.ds(b, 1), :] = jnp.sum(low.astype(F32), axis=0, keepdims=True)
        grads[pl.ds(0, 768), cols] = dot(codebook_t[...], low)
        grads[pl.ds(768, 256), cols] = dot(hidden_t[rows(b * 256, 256), :], code_low[...])

    wires = Wires(wire_s, wire_r)
    chunks = []

    def tick():
        if chunks:
            k, i = chunks.pop(0)
            answers.start(k, i, i + PACE)

    flows = [Flow(q, wires, grads, out, bufs[:6], tick) for q in range(FLOWS)]
    for q in range(2):
        gradient(2 - 2 * c + q)
    for flow in flows:
        flow.swap()
    for k in range(1, GROUPS):
        answers.start(k)
    for q in range(2):
        gradient(2 * c + q)

    def chosen(b):
        answers.arrived(b)
        part = halves(recv_b[b].reshape(256, 256))
        for i in range(4):
            here = pl.ds(i * 256, 256)
            slot, place = slot_col[here, :], slots_of(b, (256, 256), 1)
            hot = jnp.concatenate(
                [one_hot(slot == place[:, k * 128 : k * 128 + 128]) for k in range(2)], axis=1
            )
            total = joined(dot(hot, part))
            if b:
                total = total + latent_grad[here, :]
            if b == GROUPS - 1:
                total = cotangent[here, :] - 0.25 * (total - latents[here, :])
            latent_grad[here, :] = total

    picked = {8: [0], 9: [1, 2], 10: [3, 4], 11: [5, 6], 12: [7]}
    running = []
    waiting = [side_steps(wires, side, side_out, bufs[6:])] + [flow.steps() for flow in flows]
    joins = {0: 3}
    turn = 0
    while running or waiting or turn <= max(picked):
        for _ in range(joins.get(turn, 0)):
            running.append(waiting.pop(0))
        for flow in list(running):
            if next(flow, flow) is flow:
                running.remove(flow)
            tick()
        for b in picked.get(turn, []):
            while chunks and chunks[0][0] <= b:
                tick()
            chosen(b)
        turn += 1
    wires.drain()
    for exchange in (names, forth, answers):
        exchange.drain()
    for copy in aside:
        copy.wait_send()
    assert wires.used == AR_WIRES, wires.used


def whole(codebook, weight_in, bias_in, weight_out, bias_out, latents, cotangent, owner, code):
    vmem, anywhere = (pl.BlockSpec(memory_space=m) for m in (pltpu.VMEM, pl.ANY))
    dma, plain = pltpu.SemaphoreType.DMA, pltpu.SemaphoreType.REGULAR
    scratch = [
        pltpu.VMEM((1024, 768), BF16),
        pltpu.VMEM((768, 1024), BF16),
        pltpu.VMEM((1024, 256), BF16),
        pltpu.VMEM((1024, 256), F32),
        pltpu.VMEM((1024, 256), F32),
        pltpu.VMEM((1024, 128), F32),
        pltpu.VMEM((1024, 512), BF16),
    ]
    scratch += [pltpu.VMEM((GROUPS, CODES, CAP, 256), F32)] * 4
    scratch += [pltpu.VMEM((GROUPS, CODES, 1, 128), F32)] * 2
    scratch += [pltpu.VMEM((1, CODES, 1, 128), F32)] * 2
    scratch += [
        pltpu.VMEM((1024, 1024), F32),
        pltpu.VMEM((1024, 1024), BF16),
        pltpu.VMEM((768, 1024), BF16),
        pltpu.VMEM((256, 1024), BF16),
        pltpu.VMEM((1024, 512), BF16),
        pltpu.VMEM((1024, 256), F32),
        pltpu.VMEM((GROUPS, 1024, 256), BF16),
        pltpu.VMEM((1024, 256), BF16),
        pltpu.VMEM((1024, 1024), F32),
        pltpu.VMEM((8, 256), F32),
        dma((5,)),
        *[dma((GROUPS,))] * 8,
        plain, plain,
        dma((AR_WIRES,)), dma((AR_WIRES,)),
    ]
    return pl.pallas_call(
        whole_kernel,
        out_shape=(
            pltpu.VMEM((1024, 256), F32),
            pltpu.VMEM((1024, 1024), F32),
            pltpu.VMEM((8, 256), F32),
        ),
        in_specs=[anywhere, anywhere, vmem, anywhere, vmem, anywhere, anywhere, vmem, vmem],
        out_specs=(vmem, vmem, vmem),
        scratch_shapes=scratch + AR_BUFS,
        compiler_params=pltpu.CompilerParams(
            collective_id=1, has_side_effects=True, vmem_limit_bytes=52 * 2**20
        ),
    )(codebook, weight_in, bias_in, weight_out, bias_out, latents, cotangent, owner, code)


def finish_kernel(latent_grad, grads, side, latent_out, in_out, bias_in_out, w_out, bias_out, sems):
    copies = [
        pltpu.make_async_copy(latent_grad, latent_out, sems.at[0]),
        pltpu.make_async_copy(grads.at[pl.ds(0, 768)], in_out, sems.at[1]),
    ]
    for j in range(4):
        piece = pl.ds(j * 256, 256)
        copies.append(
            pltpu.make_async_copy(grads.at[pl.ds(768, 256), piece], w_out.at[piece], sems.at[2 + j])
        )
    for copy in copies:
        copy.start()
    for j in range(4):
        bias_in_out[:, j * 256 : j * 256 + 256] = side[j : j + 1, :]
    bias_out[...] = side[4:5, :]
    for copy in copies:
        copy.wait()


def finish(latent_grad, grads, side):
    vmem, anywhere = (pl.BlockSpec(memory_space=m) for m in (pltpu.VMEM, pl.ANY))
    return pl.pallas_call(
        finish_kernel,
        out_shape=tuple(
            jax.ShapeDtypeStruct(shape, F32)
            for shape in ((1024, 256), (768, 1024), (1, 1024), (1024, 256), (1, 256))
        ),
        in_specs=[vmem, vmem, vmem],
        out_specs=(anywhere, anywhere, vmem, anywhere, vmem),
        scratch_shapes=[pltpu.SemaphoreType.DMA((6,))],
        compiler_params=pltpu.CompilerParams(vmem_limit_bytes=16 * 2**20),
    )(latent_grad, grads, side)


def per_device(
    codebook, weight_in, bias_in, weight_out, bias_out, latents, cotangent, code_owner, code_row
):
    parts = whole(
        codebook, weight_in, bias_in[None], weight_out, bias_out[None], latents, cotangent,
        code_owner.reshape(1, 1024), code_row.reshape(1, 1024),
    )
    latent_grad, gw_in, gb_in, gw_out, gb_out = finish(*parts)
    return (latent_grad, gw_in, gb_in[0], gw_out, gb_out[0])


def solution(mesh):
    placed = (
        P(("code", "dp"), None),
        P(),
        P(),
        P(),
        P(),
        P(("code", "dp"), None),
        P(("code", "dp"), None),
        P(("code", "dp"), None),
        P(("code", "dp")),
    )
    return jax.shard_map(
        per_device,
        mesh=mesh,
        in_specs=placed,
        out_specs=(P(("code", "dp"), None), P(), P(), P(), P()),
        check_vma=False,
    )
```

```python
import jax
import jax.numpy as jnp
from jax import lax
from jax.experimental import pallas as pl
from jax.experimental.pallas import tpu as pltpu
from jax.sharding import PartitionSpec as P

scale_gelu = 0.7978845608028654
cubic_term = 0.044715


MESH = pl.DeviceIdType.MESH
NX, NY, NZ = 4, 4, 8
CAP, DEVICES, GROUPS, CODES = 8, 256, 8, 32
PACE = 4
LANES = 256
F32, BF16 = jnp.float32, jnp.bfloat16


def rows(start, size):
    return pl.ds(pl.multiple_of(start, 8), size)


class Wires:
    def __init__(self, send, recv):
        self.send, self.recv, self.used, self.open = send, recv, 0, []

    def start(self, src, dst, to):
        k = self.used
        self.used += 1
        copy = pltpu.make_async_remote_copy(
            src_ref=src,
            dst_ref=dst,
            send_sem=self.send.at[k],
            recv_sem=self.recv.at[k],
            device_id=to,
            device_id_type=MESH,
        )
        copy.start()
        self.open.append(copy)
        return copy

    def drain(self):
        for copy in self.open:
            copy.wait_send()


FLOWS = 512 // LANES
AR_WIRES = FLOWS * (4 + 6 + 3 + 7 + 7 + 3 + 6 + 5) + 14


def position():
    code, dp = lax.axis_index("code"), lax.axis_index("dp")
    return lax.div(dp, 2), lax.div(code, NZ), lax.rem(code, NZ), lax.rem(dp, 2)


def device(x, y, z, c):
    return (y * NZ + z, x * 2 + c)


class Ring:
    def __init__(self, wires, spot, right, left, size):
        self.w, self.p, self.n = wires, spot, size
        self.right, self.left = right, left
        self.h = size // 2

    def chunk(self, step):
        return lax.rem(self.p + step, 4) * self.n

    def scatter_start(self, acc, base, mid, edge):
        n, h, w = self.n, self.h, self.w
        self.acc, self.base, self.mid, self.edge = acc, base, mid, edge
        far, nxt, prv = (base + self.chunk(s) for s in (2, 1, 3))
        self.nxt, self.prv = nxt, prv
        self.far_a = w.start(acc.at[rows(far, h)], mid.at[0], self.right)
        self.far_b = w.start(acc.at[rows(far + h, h)], mid.at[1], self.left)
        self.near_b = w.start(acc.at[rows(nxt + h, h)], edge.at[0, pl.ds(h, h)], self.right)
        self.near_a = w.start(acc.at[rows(prv, h)], edge.at[1, pl.ds(0, h)], self.left)

    def scatter_mid(self):
        h, w, acc = self.h, self.w, self.acc
        self.far_a.wait_recv()
        here = rows(self.nxt, h)
        acc[here, :] = acc[here, :] + self.mid[0]
        self.pass_a = w.start(acc.at[here], self.edge.at[0, pl.ds(0, h)], self.right)
        self.far_b.wait_recv()
        here = rows(self.prv + h, h)
        acc[here, :] = acc[here, :] + self.mid[1]
        self.pass_b = w.start(acc.at[here], self.edge.at[1, pl.ds(h, h)], self.left)

    def scatter_end(self):
        for copy in (self.near_b, self.near_a, self.pass_a, self.pass_b):
            copy.wait_recv()
        mine = self.base + self.chunk(0)
        here = rows(mine, self.n)
        self.acc[here, :] = self.acc[here, :] + (self.edge[0] + self.edge[1])
        return mine

    def gather_start(self, out, base, cols):
        h, w = self.h, self.w
        self.out, self.base, self.cols = out, base, cols
        mine = base + self.chunk(0)
        first, second = (out.at[rows(mine + s, h), cols] for s in (0, h))
        self.right_a = w.start(first, first, self.right)
        self.left_b = w.start(second, second, self.left)
        self.right_b = w.start(second, second, self.right)
        self.left_a = w.start(first, first, self.left)

    def gather_mid(self):
        h, w, out = self.h, self.w, self.out
        self.right_a.wait_recv()
        part = out.at[rows(self.base + self.chunk(3), h), self.cols]
        self.on_a = w.start(part, part, self.right)
        self.left_b.wait_recv()
        part = out.at[rows(self.base + self.chunk(1) + h, h), self.cols]
        self.on_b = w.start(part, part, self.left)

    def gather_near(self):
        self.right_b.wait_recv()
        self.left_a.wait_recv()


class Direct:
    def __init__(self, wires, spot, peers, size):
        self.w, self.p, self.peers, self.n = wires, spot, peers, size

    def chunk(self, step):
        return lax.rem(self.p + step, 4) * self.n

    def scatter_start(self, acc, base, edge):
        self.acc, self.base, self.edge = acc, base, edge
        self.copies = [
            self.w.start(acc.at[rows(base + self.chunk(r), self.n)], edge.at[r - 1], to)
            for r, to in zip((1, 2, 3), self.peers)
        ]

    def scatter_end(self):
        for copy in self.copies:
            copy.wait_recv()
        mine = self.base + self.chunk(0)
        here = rows(mine, self.n)
        total = (self.edge[0] + self.edge[1]) + self.edge[2]
        self.acc[here, :] = self.acc[here, :] + total
        return mine

    def gather_start(self, out, base, cols):
        part = out.at[rows(base + self.chunk(0), self.n), cols]
        self.copies = [self.w.start(part, part, to) for to in self.peers]

    def gather_end(self):
        for copy in self.copies:
            copy.wait_recv()


ORDER = (2, 1, 3, 0)


class Flow:
    def __init__(self, q, wires, grads, out, bufs, tick):
        self.q, self.w, self.grads, self.out = q, wires, grads, out
        self.tick = tick
        acc, half, mid1, edge1, edge2, deep = bufs
        self.acc, self.half, self.deep = acc.at[q], half.at[q], deep.at[q]
        self.outer_bufs = mid1.at[q], edge1.at[q]
        self.inner_buf = edge2.at[q]
        x, y, z, c = position()
        self.z, self.other = z, device(x, y, z, 1 - c)
        self.columns = [device(x, y, lax.rem(z + r, NZ), c) for r in range(1, NZ)]
        along_x = x, [device(lax.rem(x + s, NX), y, z, c) for s in (1, 2, 3)]
        along_y = y, [device(x, lax.rem(y + s, NY), z, c) for s in (1, 2, 3)]
        first, second = (along_x, along_y) if q % 2 == 0 else (along_y, along_x)
        self.outer = Ring(wires, first[0], first[1][0], first[1][2], 256)
        self.inner = Direct(wires, *second, 64)
        place = (q % 2) * 256 + (q // 2) * LANES
        self.cols = pl.ds(pl.multiple_of(c * 512 + place, LANES), LANES)
        self.away = pl.ds(pl.multiple_of(512 - c * 512 + place, LANES), LANES)

    def swap(self):
        self.swaps = []
        for step in ORDER:
            here = rows(self.outer.chunk(step), 256)
            self.swaps.append(
                self.w.start(self.grads.at[here, self.away], self.half.at[here], self.other)
            )

    def back(self, start, size):
        part = self.out.at[rows(start, size), self.cols]
        self.backs.append(self.w.start(part, part, self.other))

    def steps(self):
        outer, inner, acc, z = self.outer, self.inner, self.acc, self.z
        for copy, step in zip(self.swaps, ORDER):
            here = rows(outer.chunk(step), 256)
            copy.wait_recv()
            acc[here, :] = self.grads[here, self.cols] + self.half[here, :]
            self.tick()
        outer.scatter_start(acc, 0, *self.outer_bufs)
        yield
        outer.scatter_mid()
        yield
        first = outer.scatter_end()
        inner.scatter_start(acc, first, self.inner_buf)
        yield
        second = inner.scatter_end()
        downs = []
        for r in range(1, NZ):
            part = acc.at[rows(second + lax.rem(z + r, NZ) * 8, 8)]
            downs.append(self.w.start(part, self.deep.at[r - 1], self.columns[r - 1]))
        yield
        for copy in downs:
            copy.wait_recv()
        here = rows(second + z * 8, 8)
        total = acc[here, :]
        for r in range(NZ - 1):
            total = total + self.deep[r]
        self.out[here, self.cols] = total
        part = self.out.at[here, self.cols]
        ups = [self.w.start(part, part, to) for to in self.columns]
        yield
        for copy in ups:
            copy.wait_recv()
        inner.gather_start(self.out, first, self.cols)
        yield
        inner.gather_end()
        self.backs = []
        outer.gather_start(self.out, 0, self.cols)
        self.back(outer.chunk(0), 256)
        yield
        outer.gather_mid()
        yield
        outer.gather_near()
        self.back(outer.chunk(3), 256)
        self.back(outer.chunk(1), 256)
        yield
        outer.on_a.wait_recv()
        self.back(outer.chunk(2), 128)
        outer.on_b.wait_recv()
        self.back(outer.chunk(2) + 128, 128)
        yield
        for copy in self.backs:
            copy.wait_recv()


def side_steps(wires, side, side_out, bufs):
    side0, side1, side2, side3 = bufs
    x, y, z, c = position()
    copy = wires.start(side, side0, device(x, y, z, 1 - c))
    yield
    copy.wait_recv()
    side1[x] = side[...] + side0[...]
    sides = [
        wires.start(side1.at[x], side1.at[x], device(lax.rem(x + r, NX), y, z, c))
        for r in range(1, NX)
    ]
    yield
    for copy in sides:
        copy.wait_recv()
    side2[y] = (side1[0] + side1[1]) + (side1[2] + side1[3])
    sides = [
        wires.start(side2.at[y], side2.at[y], device(x, lax.rem(y + r, NY), z, c))
        for r in range(1, NY)
    ]
    yield
    for copy in sides:
        copy.wait_recv()
    side3[z] = (side2[0] + side2[1]) + (side2[2] + side2[3])
    sides = [
        wires.start(side3.at[z], side3.at[z], device(x, y, lax.rem(z + r, NZ), c))
        for r in range(1, NZ)
    ]
    yield
    yield
    for copy in sides:
        copy.wait_recv()
    total = side3[0]
    for r in range(1, NZ):
        total = total + side3[r]
    side_out[...] = total


AR_BUFS = [
    pltpu.VMEM((FLOWS, 1024, LANES), F32),
    pltpu.VMEM((FLOWS, 1024, LANES), F32),
    pltpu.VMEM((FLOWS, 2, 128, LANES), F32),
    pltpu.VMEM((FLOWS, 2, 256, LANES), F32),
    pltpu.VMEM((FLOWS, 3, 64, LANES), F32),
    pltpu.VMEM((FLOWS, 7, 8, LANES), F32),
    pltpu.VMEM((8, 256), F32),
    pltpu.VMEM((4, 8, 256), F32),
    pltpu.VMEM((4, 8, 256), F32),
    pltpu.VMEM((8, 8, 256), F32),
]


def greet(peers, sem):
    for peer in peers:
        pl.semaphore_signal(sem, inc=1, device_id=peer, device_id_type=MESH)


def owner_dp(group, forth=1):
    x, _, _, c = position()
    across = lax.rem(x + (NX + forth * (group // 2)), NX)
    return across * 2 + lax.rem(c + group % 2, 2)


class Exchange:
    def __init__(self, source, target, send, recv, forth):
        self.source, self.target, self.forth = source, target, forth
        self.send, self.recv, self.all = send, recv, []
        _, y, z, _ = position()
        self.y, self.z, self.me = y, z, y * NZ + z

    def start(self, group, begin=0, end=CODES):
        dp = owner_dp(group, self.forth)
        source, target = self.source.at[group], self.target.at[group]

        def copy(code, src, dst):
            return pltpu.make_async_remote_copy(
                src_ref=src,
                dst_ref=dst,
                send_sem=self.send.at[group],
                recv_sem=self.recv.at[group],
                device_id=(code, dp),
                device_id_type=MESH,
            )

        def one(i, carry):
            code = lax.rem(self.y + lax.div(i, NZ), NY) * NZ + lax.rem(self.z + lax.rem(i, NZ), NZ)
            copy(code, source.at[code], target.at[self.me]).start()
            return carry

        own = 1 if group == 0 else 0
        lax.fori_loop(max(own, begin), end, one, 0)
        if begin:
            return
        if own:
            self.target[group, self.me] = self.source[group, self.me]
        whole = pl.ds(0, CODES - own)
        near = self.y * NZ + lax.rem(self.z + 1, NZ)
        self.all.append(copy(near, source.at[whole], target.at[whole]))

    def arrived(self, group):
        self.all[group].wait_recv()

    def drain(self):
        for copy in self.all:
            copy.wait_send()


def dot(a, b):
    return jnp.dot(a, b, preferred_element_type=F32)


def halves(value):
    high = value.astype(BF16)
    low = (value - high.astype(F32)).astype(BF16)
    return jnp.concatenate([high, low], axis=1)


def joined(value):
    return value[:, :256] + value[:, 256:]


def upright(row):
    return jnp.transpose(jnp.broadcast_to(row, (128, row.shape[1])))


def iota(shape, dim):
    return lax.broadcasted_iota(jnp.int32, shape, dim)


def one_hot(condition):
    return jnp.where(condition, 1.0, 0.0).astype(BF16)


def slots_of(group, shape, dim):
    place = iota(shape, dim)
    slot = (place // CAP) * (GROUPS * CAP) + place % CAP + owner_dp(group) * CAP
    return slot.astype(F32)


def whole_kernel(
    codebook_h, weight_in_h, bias_in, weight_out_h, bias_out, latents_h, cotangent_h, owner, code,
    latent_grad, out, side_out,
    codebook, weight_in, weight_out, latents, cotangent, slot_col, values, send_a, recv_a, send_b,
    recv_b, ids_out, ids_mid, ids_sum, ids_in, slope, hidden_t, codebook_t, weight_out_t, projected, base, picks,
    code_low, grads, side,
    load, ids_s, ids_r, c_s, c_r, a_s, a_r, b_s, b_r, near_a, near_b, wire_s, wire_r, *bufs,
):
    x, y, z, c = position()
    pairs = (
        (latents_h, latents), (cotangent_h, cotangent), (codebook_h, codebook),
        (weight_in_h, weight_in), (weight_out_h, weight_out),
    )
    loads = [pltpu.make_async_copy(src, dst, load.at[i]) for i, (src, dst) in enumerate(pairs)]
    for copy in loads:
        copy.start()
    barrier = pltpu.get_barrier_semaphore()
    row_peers = [
        device(lax.rem(x + r, NX), y, z, lax.rem(c + s, 2))
        for r in range(NX) for s in range(2) if r + s
    ]
    y_peers = [device(x, lax.rem(y + r, NY), z, c) for r in range(1, NY)]
    z_peers = [device(x, y, lax.rem(z + r, NZ), c) for r in range(1, NZ)]
    line_peers = row_peers + y_peers + z_peers
    greet(line_peers, barrier)

    owner_row = owner[...].astype(F32)
    code_row = code[...].astype(F32) + 1.0
    owner_col = upright(owner_row)
    lower = iota((128, 128), 0) < iota((128, 128), 1)
    ranks = []
    for i in range(8):
        name = owner_row[:, 128 * i : 128 * i + 128]
        count = jnp.where((owner_col[128 * i : 128 * i + 128] == name) & lower, 1.0, 0.0)
        for j in range(i):
            count += jnp.where(owner_col[128 * j : 128 * j + 128] == name, 1.0, 0.0)
        ranks.append(jnp.sum(count, axis=0, keepdims=True))
    rank_row = jnp.concatenate(ranks, axis=1)
    slot_row = owner_row * CAP + rank_row
    slot_col[...] = upright(slot_row)
    pl.semaphore_wait(barrier, len(line_peers))
    greet(y_peers, near_a)

    rank_col = upright(rank_row)
    code_col = upright(code_row)
    code_high = jnp.floor(code_col * (1.0 / 32))
    lane = iota((1024, 128), 1)
    mine = (rank_col == (lane % CAP).astype(F32)) & (lane < GROUPS * CAP)
    digits = jnp.concatenate(
        [
            jnp.where(mine, code_high, 0.0).astype(BF16),
            jnp.where(mine, code_col - 32.0 * code_high, 0.0).astype(BF16),
        ],
        axis=1,
    )
    place = iota((256, 1024), 0)
    group = place // CODES
    across = (x + group // 2) % NX * 2 + (c + group % 2) % 2
    named = dot(one_hot(owner_row == ((place % CODES) * GROUPS + across).astype(F32)), digits)
    named = named[:, :128] * 32.0 + named[:, 128:]
    ours = iota((256, 128), 1) // CAP == iota((256, 128), 0) // CODES
    ids_out[...] = jnp.where(ours, named, 0.0).reshape(GROUPS, CODES, 1, 128)
    aside = []
    for b in range(1, GROUPS):
        aside.append(
            pltpu.make_async_remote_copy(
                src_ref=ids_out.at[b],
                dst_ref=ids_mid.at[b],
                send_sem=ids_s.at[b],
                recv_sem=ids_r.at[b],
                device_id=(y * NZ + z, owner_dp(b)),
                device_id_type=MESH,
            )
        )
        aside[-1].start()
    loads[0].wait()
    loads[1].wait()
    values[pl.ds(0, 1024), :] = halves(cotangent[...] - latents[...])
    pl.semaphore_wait(near_a, len(y_peers))
    greet(row_peers, near_b)

    names = Exchange(ids_sum, ids_in, c_s, c_r, 1)
    forth = Exchange(send_a, recv_a, a_s, a_r, 1)
    answers = Exchange(send_b, recv_b, b_s, b_r, -1)
    for b in range(GROUPS):
        hot = one_hot(slot_row == slots_of(b, (256, 1024), 0))
        block = joined(dot(hot, values[pl.ds(0, 1024), :]))
        send_a[b] = block.reshape(CODES, CAP, 256)
        if b == 1:
            pl.semaphore_wait(near_b, len(row_peers))
        forth.start(b)
        if b == 1:
            total = ids_out[0]
            for k in range(1, GROUPS):
                aside[k - 1].wait_recv()
                total = total + ids_mid[k]
            ids_sum[0] = total
            names.start(0)

    for copy in loads[2:]:
        copy.wait()
    weight_out_t[...] = jnp.transpose(weight_out[...].astype(F32)).astype(BF16)

    def forward(i, carry):
        here = rows(i * 256, 256)
        block = codebook[here, :]
        pre = dot(block, weight_in[...]) + bias_in[...]
        tangent = jnp.tanh(scale_gelu * (pre + cubic_term * pre * pre * pre))
        value = 0.5 * pre * (1.0 + tangent)
        slope[here, :] = 0.5 * (1.0 + tangent) + 0.5 * pre * (
            1.0 - tangent * tangent
        ) * scale_gelu * (1.0 + 3.0 * cubic_term * pre * pre)
        hidden = value.astype(BF16)
        cols = pl.ds(pl.multiple_of(i * 256, 256), 256)
        hidden_t[:, cols] = jnp.transpose(value).astype(BF16)
        codebook_t[:, cols] = jnp.transpose(block.astype(F32)).astype(BF16)
        block = dot(hidden, weight_out[...]) + bias_out[...]
        base[here, :] = block
        projected[here, :] = halves(block)
        return carry

    lax.fori_loop(0, 4, forward, 0)

    names.arrived(0)
    ones = jnp.ones((256, 128), BF16)
    for b in range(GROUPS):
        ids = ids_in[0]
        own = iota((256, 128), 0) % CAP + b * CAP == iota((256, 128), 1)
        ids = jnp.broadcast_to(ids, (CODES, CAP, 128)).reshape(256, 128)
        ids = jnp.where(own, ids, 0.0)
        ids_col = jnp.sum(ids, axis=1, keepdims=True)
        ids_row = jnp.sum(jnp.transpose(ids), axis=0, keepdims=True)
        hot = one_hot(ids_col == (iota((256, 1024), 1) + 1).astype(F32))
        send_b[b] = joined(dot(hot, projected[...])).reshape(CODES, CAP, 256)
        for i in range(4):
            hot = one_hot(ids_row == (iota((256, 256), 0) + (256 * i + 1)).astype(F32))
            picks[b, pl.ds(i * 256, 256), :] = hot
    for i in range(4):
        here = pl.ds(i * 256, 256)
        count = dot(picks[0, here, :], ones)
        for j in range(1, GROUPS):
            count += dot(picks[j, here, :], ones)
        base[here, :] = base[here, :] * jnp.concatenate([count, count], axis=1)

    for b in range(GROUPS):
        forth.arrived(b)
        if 4 <= b < 7:
            answers.start(b - 4)
        part = halves(recv_a[b].reshape(256, 256))
        for i in range(4):
            here = pl.ds(i * 256, 256)
            base[here, :] = base[here, :] + joined(dot(picks[b, here, :], part))
    code_low[...] = base[...].astype(BF16)
    side[...] = jnp.zeros((8, 256), F32)
    side[4:5, :] = jnp.sum(base[...], axis=0, keepdims=True)

    def gradient(b):
        cols = pl.ds(pl.multiple_of(b * 256, 256), 256)
        back = dot(code_low[...], weight_out_t[:, cols])
        low = (back * slope[:, cols]).astype(BF16)
        side[pl.ds(b, 1), :] = jnp.sum(low.astype(F32), axis=0, keepdims=True)
        grads[pl.ds(0, 768), cols] = dot(codebook_t[...], low)
        grads[pl.ds(768, 256), cols] = dot(hidden_t[rows(b * 256, 256), :], code_low[...])

    wires = Wires(wire_s, wire_r)
    chunks = []

    def tick():
        if chunks:
            k, i = chunks.pop(0)
            answers.start(k, i, i + PACE)

    flows = [Flow(q, wires, grads, out, bufs[:6], tick) for q in range(FLOWS)]
    for q in range(2):
        gradient(2 - 2 * c + q)
    for flow in flows:
        flow.swap()
    for k in range(3, GROUPS):
        answers.start(k)
    for q in range(2):
        gradient(2 * c + q)

    def chosen(b):
        answers.arrived(b)
        part = halves(recv_b[b].reshape(256, 256))
        for i in range(4):
            here = pl.ds(i * 256, 256)
            slot, place = slot_col[here, :], slots_of(b, (256, 256), 1)
            hot = jnp.concatenate(
                [one_hot(slot == place[:, k * 128 : k * 128 + 128]) for k in range(2)], axis=1
            )
            total = joined(dot(hot, part))
            if b:
                total = total + latent_grad[here, :]
            if b == GROUPS - 1:
                total = cotangent[here, :] - 0.25 * (total - latents[here, :])
            latent_grad[here, :] = total

    picked = {8: [0], 9: [1, 2], 10: [3, 4], 11: [5, 6], 12: [7]}
    running = []
    waiting = [side_steps(wires, side, side_out, bufs[6:])] + [flow.steps() for flow in flows]
    joins = {0: 3}
    turn = 0
    while running or waiting or turn <= max(picked):
        for _ in range(joins.get(turn, 0)):
            running.append(waiting.pop(0))
        for flow in list(running):
            if next(flow, flow) is flow:
                running.remove(flow)
            tick()
        for b in picked.get(turn, []):
            while chunks and chunks[0][0] <= b:
                tick()
            chosen(b)
        turn += 1
    wires.drain()
    for exchange in (names, forth, answers):
        exchange.drain()
    for copy in aside:
        copy.wait_send()
    assert wires.used == AR_WIRES, wires.used


def whole(codebook, weight_in, bias_in, weight_out, bias_out, latents, cotangent, owner, code):
    vmem, anywhere = (pl.BlockSpec(memory_space=m) for m in (pltpu.VMEM, pl.ANY))
    dma, plain = pltpu.SemaphoreType.DMA, pltpu.SemaphoreType.REGULAR
    scratch = [
        pltpu.VMEM((1024, 768), BF16),
        pltpu.VMEM((768, 1024), BF16),
        pltpu.VMEM((1024, 256), BF16),
        pltpu.VMEM((1024, 256), F32),
        pltpu.VMEM((1024, 256), F32),
        pltpu.VMEM((1024, 128), F32),
        pltpu.VMEM((1024, 512), BF16),
    ]
    scratch += [pltpu.VMEM((GROUPS, CODES, CAP, 256), F32)] * 4
    scratch += [pltpu.VMEM((GROUPS, CODES, 1, 128), F32)] * 2
    scratch += [pltpu.VMEM((1, CODES, 1, 128), F32)] * 2
    scratch += [
        pltpu.VMEM((1024, 1024), F32),
        pltpu.VMEM((1024, 1024), BF16),
        pltpu.VMEM((768, 1024), BF16),
        pltpu.VMEM((256, 1024), BF16),
        pltpu.VMEM((1024, 512), BF16),
        pltpu.VMEM((1024, 256), F32),
        pltpu.VMEM((GROUPS, 1024, 256), BF16),
        pltpu.VMEM((1024, 256), BF16),
        pltpu.VMEM((1024, 1024), F32),
        pltpu.VMEM((8, 256), F32),
        dma((5,)),
        *[dma((GROUPS,))] * 8,
        plain, plain,
        dma((AR_WIRES,)), dma((AR_WIRES,)),
    ]
    return pl.pallas_call(
        whole_kernel,
        out_shape=(
            pltpu.VMEM((1024, 256), F32),
            pltpu.VMEM((1024, 1024), F32),
            pltpu.VMEM((8, 256), F32),
        ),
        in_specs=[anywhere, anywhere, vmem, anywhere, vmem, anywhere, anywhere, vmem, vmem],
        out_specs=(vmem, vmem, vmem),
        scratch_shapes=scratch + AR_BUFS,
        compiler_params=pltpu.CompilerParams(
            collective_id=1, has_side_effects=True, vmem_limit_bytes=52 * 2**20
        ),
    )(codebook, weight_in, bias_in, weight_out, bias_out, latents, cotangent, owner, code)


def finish_kernel(latent_grad, grads, side, latent_out, in_out, bias_in_out, w_out, bias_out, sems):
    copies = [
        pltpu.make_async_copy(latent_grad, latent_out, sems.at[0]),
        pltpu.make_async_copy(grads.at[pl.ds(0, 768)], in_out, sems.at[1]),
    ]
    for j in range(4):
        piece = pl.ds(j * 256, 256)
        copies.append(
            pltpu.make_async_copy(grads.at[pl.ds(768, 256), piece], w_out.at[piece], sems.at[2 + j])
        )
    for copy in copies:
        copy.start()
    for j in range(4):
        bias_in_out[:, j * 256 : j * 256 + 256] = side[j : j + 1, :]
    bias_out[...] = side[4:5, :]
    for copy in copies:
        copy.wait()


def finish(latent_grad, grads, side):
    vmem, anywhere = (pl.BlockSpec(memory_space=m) for m in (pltpu.VMEM, pl.ANY))
    return pl.pallas_call(
        finish_kernel,
        out_shape=tuple(
            jax.ShapeDtypeStruct(shape, F32)
            for shape in ((1024, 256), (768, 1024), (1, 1024), (1024, 256), (1, 256))
        ),
        in_specs=[vmem, vmem, vmem],
        out_specs=(anywhere, anywhere, vmem, anywhere, vmem),
        scratch_shapes=[pltpu.SemaphoreType.DMA((6,))],
        compiler_params=pltpu.CompilerParams(vmem_limit_bytes=16 * 2**20),
    )(latent_grad, grads, side)


def per_device(
    codebook, weight_in, bias_in, weight_out, bias_out, latents, cotangent, code_owner, code_row
):
    parts = whole(
        codebook, weight_in, bias_in[None], weight_out, bias_out[None], latents, cotangent,
        code_owner.reshape(1, 1024), code_row.reshape(1, 1024),
    )
    latent_grad, gw_in, gb_in, gw_out, gb_out = finish(*parts)
    return (latent_grad, gw_in, gb_in[0], gw_out, gb_out[0])


def solution(mesh):
    placed = (
        P(("code", "dp"), None),
        P(),
        P(),
        P(),
        P(),
        P(("code", "dp"), None),
        P(("code", "dp"), None),
        P(("code", "dp"), None),
        P(("code", "dp")),
    )
    return jax.shard_map(
        per_device,
        mesh=mesh,
        in_specs=placed,
        out_specs=(P(("code", "dp"), None), P(), P(), P(), P()),
        check_vma=False,
    )
```
